32 devices in a mesh: dp: 16 (over z, y, x), tensor: 2 (over core).
Axes of the slice: x: 2, y: 2, z: 4, core: 2. Of those that a mesh axis runs over, the one named last changes fastest.
Arguments:
- block_input: bfloat16 [8192, 1536], P(('dp', 'tensor')), may hold values from -6 to 6
- teacher: bfloat16 [8192, 1536], P(('dp', 'tensor')), may hold values from -6 to 6
- lengths: int32 [16], replicated, may hold values from 256 to 512, as said below
- routes: int32 [8192, 6], P('dp'), may hold values from 0 to 15, all different within a row; in each aligned block of 256 rows (0 to 255, 256 to 511, ...) at most 128 rows name the same one
- gain_attn: float32 [1536], replicated, may hold values from 0.5 to 1.5
- w_query: bfloat16 [1536, 1536], P('dp', 'tensor'), may hold values from -0.15625 to 0.15625
- key_value_weight: bfloat16 [2, 1536, 512], P(None, 'dp', 'tensor'), may hold values from -0.15625 to 0.15625
- w_out: bfloat16 [1536, 1536], P('dp', 'tensor'), may hold values from -1.75 to 1.75
- gain_moe: float32 [1536], replicated, may hold values from 0.5 to 1.5
- w_router: bfloat16 [1536, 16], P('dp'), may hold values from -0.078125 to 0.078125
- w_shared_in: bfloat16 [2, 1536, 1024], P(None, 'dp', 'tensor'), may hold values from -0.15625 to 0.15625
- w_shared_out: bfloat16 [1536, 1024], P('dp', 'tensor'), may hold values from -0.25 to 0.25
- w_expert_in: bfloat16 [16, 2, 1536, 512], P('dp', None, None, 'tensor'), may hold values from -0.15625 to 0.15625
- w_expert_out: bfloat16 [16, 1536, 512], P('dp', None, 'tensor'), may hold values from -0.5 to 0.5
Outputs:
- block_output: bfloat16 [8192, 1536], P(('dp', 'tensor'))
- loss: float32 [], replicated
- input_grad: float32 [8192, 1536], P(('dp', 'tensor'))
- grad_gain_attn: float32 [1536], replicated
- grad_w_query: float32 [1536, 1536], P('dp', 'tensor')
- grad_w_kv: float32 [2, 1536, 512], P(None, 'dp', 'tensor')
- grad_w_out: float32 [1536, 1536], P('dp', 'tensor')
- grad_gain_moe: float32 [1536], replicated
- grad_w_router: float32 [1536, 16], P('dp')
- grad_w_shared_in: float32 [2, 1536, 1024], P(None, 'dp', 'tensor')
- grad_w_shared_out: float32 [1536, 1024], P('dp', 'tensor')
- grad_w_expert_in: float32 [16, 2, 1536, 512], P('dp', None, None, 'tensor')
- grad_w_expert_out: float32 [16, 1536, 512], P('dp', None, 'tensor')
The draws below stay inside these ranges and needn't reach their ends.
Inputs may be any that keep to these rules, and one draw needn't show every extreme that they name: `lengths`: each sequence has at least half of its 512 slots valid; the longest has exactly 512. `routes`: the 6 experts of a row differ. Within each aligned block of 256 rows (one slice of a sequence) no expert is named by more than 128 rows, and some block has an expert named by exactly 128 rows.
All inputs are finite; a program needn't handle non-finite values.
Results may differ from the reference program's by a relative error of at most 0.018.
Values may be sent and summed in bfloat16 or wider, within the bound.
No kernel may reach another device: no remote copies, remote signals or barrier semaphores. Data moves between devices by JAX's collectives and lax.ppermute only.
A program may use at most 192 MiB of HBM per device.

```python
import math
import jax
import jax.numpy as jnp
import numpy as np
from jax import lax

MODEL_WIDTH = 1536
QUERY_HEADS = 12
KEY_VALUE_HEADS = 4
HEAD_SIZE = 128
FE = 512
FS = 1024
TOPK = 6
TOK_DEV = 256
SEQ = 512
EXPERTS = 16
CAP = 128
TOKENS = 8192
N_DP = 16
N_TENSOR = 2


def draw_lengths(key, part):
    drawn_lengths = jax.random.randint(key, (N_DP,), SEQ // 2, SEQ + 1)
    longest_at = jax.random.randint(jax.random.fold_in(key, 7), (), 0, N_DP)
    return jnp.where(jnp.arange(N_DP) == longest_at, SEQ, drawn_lengths).astype(jnp.int32)


def steps_of(key, extent, split, low, largest):
    loudness = 1.0
    for axis_at, shards_of in split:
        steps = jax.random.uniform(jax.random.fold_in(jax.random.fold_in(key, 6), axis_at), (shards_of,), jnp.float32, low / len(split), largest / len(split))
        loudness = loudness * jnp.repeat(jnp.exp(steps), extent[axis_at] // shards_of).reshape((-1,) + (1,) * (len(extent) - 1 - axis_at))
    return loudness


def assign_block(own_key, own, number, rows, number_of, top, bound, lean):
    order = jax.random.permutation(own_key, number_of)
    heavy_load, common = shares(number_of, rows * top, bound, lean, True), shares(number_of, rows * top, bound, lean, False)
    places = jnp.arange(number_of)

    def named(tallies, offset_by):
        used = int((tallies > 0).sum())
        fixed = max(1, used // 4)
        shifted = fixed + (places - fixed + offset_by * (used - fixed)) % max(1, number_of - fixed)
        return jnp.zeros((number_of,), jnp.int32).at[order[jnp.where(places < fixed, places, shifted)]].set(jnp.asarray(tallies, jnp.int32))

    tallies = jnp.where(number % 4 == 0, named(heavy_load, number // 4), named(common, number - number // 4 - 1))
    mixed = jax.random.permutation(jax.random.fold_in(own, 3), number_of)
    source_of, taker = mixed[0:number_of // 2 * 2:2], mixed[1:number_of // 2 * 2:2]
    room = jnp.minimum(tallies[source_of] - 1, bound - tallies[taker]) // 2
    room = jnp.where((source_of == order[0]) | (taker == order[0]) | (tallies[taker] == 0), 0, jnp.maximum(room, 0))
    shifted = jax.random.randint(jax.random.fold_in(own, 4), (number_of // 2,), 0, 1 << 20) % (room + 1)
    tallies = tallies.at[source_of].add(-shifted).at[taker].add(shifted)
    items = jnp.searchsorted(jnp.cumsum(tallies), jnp.arange(rows * top), side="right").astype(jnp.int32)
    listing = items.reshape(top, rows).T
    listing = listing[jax.random.permutation(jax.random.fold_in(own, 1), rows)]
    offset_by = jax.random.randint(jax.random.fold_in(own, 2), (rows, 1), 0, top)
    return jnp.take_along_axis(listing, (jnp.arange(top)[None, :] + offset_by) % top, axis=1)


def shares(amount, total, most, lean, full):
    portions = [(1 << 20) // math.isqrt(grade ** lean) + 1 for grade in range(1, amount + 1)]
    largest = most if full else min(most, max(-(-total // amount), total * portions[0] // sum(portions)))
    least = 1 if total - largest >= amount - 1 else 0
    counts, rest = [largest] + [least] * (amount - 1), total - largest - least * (amount - 1)
    while rest > 0:
        movable = [i for i in range(1, amount) if counts[i] < largest] or [i for i in range(1, amount) if counts[i] < most]
        mass, budget = sum([portions[i] for i in movable]), rest
        for i in movable:
            addition = min(most - counts[i], max(1, budget * portions[i] // mass), rest)
            counts[i] = counts[i] + addition
            rest = rest - addition
    return np.array(counts)


def gaussian(rng, dims, spread, most, pieces=(), kind=jnp.bfloat16):
    values = jax.random.normal(rng, dims, jnp.float32) * spread
    if len(pieces) > 0:
        values = steps_of(rng, dims, pieces, -0.22, 0.18) * values
    return jnp.clip(values, min=-most, max=most).astype(kind)


def setup_inputs(seed: int = 0) -> dict:
    arg_keys = jax.random.split(jax.random.key(seed), 15)
    block_input = gaussian(arg_keys[0], (TOKENS, MODEL_WIDTH), 1.0, 6.0, ((0, 32),))
    teacher = gaussian(arg_keys[1], (TOKENS, MODEL_WIDTH), 1.0, 6.0, ((0, 32),))
    lengths = draw_lengths(jax.random.fold_in(arg_keys[14], 71), 0)
    routes_keys = jax.random.split(jax.random.fold_in(arg_keys[3], 1), TOKENS // TOK_DEV)
    routes_turns = jax.random.permutation(jax.random.fold_in(arg_keys[3], 3), TOKENS // TOK_DEV)
    routes = jax.vmap(lambda own, number: assign_block(jax.random.fold_in(arg_keys[3], 2), own, number, TOK_DEV, EXPERTS, TOPK, CAP, 0))(routes_keys, routes_turns).reshape((TOKENS, TOPK))
    gain_attn = jnp.clip(1.0 + 0.1 * jax.random.normal(arg_keys[4], (MODEL_WIDTH,), jnp.float32), 0.5, 1.5)
    w_query = gaussian(arg_keys[5], (MODEL_WIDTH, QUERY_HEADS * HEAD_SIZE), MODEL_WIDTH ** -0.5, 0.15625, ((0, 16), (1, 2)))
    key_value_weight = gaussian(arg_keys[6], (2, MODEL_WIDTH, KEY_VALUE_HEADS * HEAD_SIZE), MODEL_WIDTH ** -0.5, 0.15625, ((1, 16), (2, 2)))
    w_out = gaussian(arg_keys[7], (MODEL_WIDTH, QUERY_HEADS * HEAD_SIZE), (max(1, 4 * QUERY_HEADS * HEAD_SIZE // SEQ)) ** -0.5, 1.75, ((0, 16), (1, 2)))
    gain_moe = jnp.clip(1.0 + 0.1 * jax.random.normal(arg_keys[8], (MODEL_WIDTH,), jnp.float32), 0.5, 1.5)
    w_router = gaussian(arg_keys[9], (MODEL_WIDTH, EXPERTS), (4 * MODEL_WIDTH) ** -0.5, 0.078125, ((0, 16),))
    w_shared_in = gaussian(arg_keys[10], (2, MODEL_WIDTH, FS), MODEL_WIDTH ** -0.5, 0.15625, ((1, 16), (2, 2)))
    w_shared_out = gaussian(arg_keys[11], (MODEL_WIDTH, FS), (FS // 2) ** -0.5, 0.25, ((0, 16), (1, 2)))
    w_expert_in = gaussian(arg_keys[12], (EXPERTS, 2, MODEL_WIDTH, FE), MODEL_WIDTH ** -0.5, 0.15625, ((0, 16), (3, 2)))
    w_expert_out = gaussian(arg_keys[13], (EXPERTS, MODEL_WIDTH, FE), (FE // 4) ** -0.5, 0.5, ((0, 16), (2, 2)))
    return {"block_input": block_input, "teacher": teacher, "lengths": lengths, "routes": routes, "gain_attn": gain_attn, "w_query": w_query, "key_value_weight": key_value_weight, "w_out": w_out, "gain_moe": gain_moe, "w_router": w_router, "w_shared_in": w_shared_in, "w_shared_out": w_shared_out, "w_expert_in": w_expert_in, "w_expert_out": w_expert_out}


@jax.custom_vjp
def low(v):
    return lax.optimization_barrier(v.astype(jnp.bfloat16)).astype(jnp.float32)

@jax.custom_vjp
def low_back(v):
    return v

def low_keep(v):
    return (low(v), None)

def low_pass(kept, grad):
    return (grad,)

def back_keep(v):
    return (v, None)

def back_low(kept, grad):
    return (low(grad),)
low.defvjp(low_keep, low_pass)
low_back.defvjp(back_keep, back_low)

def forward_and_back(values):
    return low_back(low(values))

def normalize(values, gain):
    row_scale = lax.rsqrt(lax.optimization_barrier(jnp.mean(values * values, axis=-1, keepdims=True)) + 1e-05)
    return values * row_scale * gain

def weight_matrix(left_side, right_side):
    return jnp.dot(left_side, right_side, precision=lax.Precision.HIGHEST)

def slot_table(route_rows, experts, capacity):
    slices = route_rows.shape[0]
    flat_routes = route_rows.reshape(slices, -1)
    one_hot = (flat_routes[:, :, None] == jnp.arange(experts, dtype=jnp.int32)[None, None, :]).astype(jnp.int32)
    within = lax.optimization_barrier(jnp.sum(jnp.cumsum(one_hot, axis=1) * one_hot, axis=-1)) - 1
    slice_ids = jnp.arange(slices, dtype=jnp.int32)[:, None]
    return (flat_routes * (slices * capacity) + slice_ids * capacity + within).reshape(-1).astype(jnp.int32)

def sequence_block(x_seq, length, route_rows, gain_attn, w_query, key_value_weight, w_out, gain_moe, w_router, w_shared_in, w_shared_out, w_expert_in, w_expert_out):
    sequence_length = x_seq.shape[0]
    positions = jnp.arange(sequence_length, dtype=jnp.int32)
    valid = (positions < length).astype(jnp.float32)[:, None]
    highest = lax.Precision.HIGHEST
    attention_normed = low(normalize(x_seq, gain_attn))
    queries = forward_and_back(weight_matrix(attention_normed, w_query)).reshape(sequence_length, QUERY_HEADS, HEAD_SIZE)
    key_row_table = forward_and_back(weight_matrix(attention_normed, key_value_weight[0])).reshape(sequence_length, KEY_VALUE_HEADS, HEAD_SIZE)
    value_row_table = forward_and_back(weight_matrix(attention_normed, key_value_weight[1])).reshape(sequence_length, KEY_VALUE_HEADS, HEAD_SIZE)
    complete_keys = jnp.repeat(key_row_table, QUERY_HEADS // KEY_VALUE_HEADS, axis=1)
    complete_values = jnp.repeat(value_row_table, QUERY_HEADS // KEY_VALUE_HEADS, axis=1)
    scores = low_back(jnp.einsum('qhd,khd->hqk', queries, complete_keys, precision=highest) * HEAD_SIZE ** (-0.5))
    allowed = (positions[None, :] <= positions[:, None]) & (positions[None, :] < length)
    scores = jnp.where(allowed[None], scores, -1e+30)
    attn_probs = low(jax.nn.softmax(scores, axis=-1))
    mixed = forward_and_back(jnp.einsum('hqk,khd->qhd', attn_probs, complete_values, precision=highest)).reshape(sequence_length, QUERY_HEADS * HEAD_SIZE)
    attn_out = low_back(weight_matrix(mixed, w_out.T))
    hidden = x_seq + attn_out
    normed_moe = low(normalize(hidden, gain_moe))
    logits = low_back(weight_matrix(normed_moe, w_router))
    chosen = jnp.take_along_axis(logits, route_rows, axis=1)
    gate_weights = jax.nn.softmax(chosen, axis=-1)
    shared_pre = low_back(jnp.einsum('td,cdf->ctf', normed_moe, w_shared_in, precision=highest))
    shared_act = low(jax.nn.silu(shared_pre[0]) * shared_pre[1])
    shared_out = weight_matrix(shared_act, w_shared_out.T)
    slot_rows = slot_table(route_rows.reshape(N_TENSOR, -1, TOPK), EXPERTS, CAP)
    buffer_size = EXPERTS * N_TENSOR * CAP
    token_ids = jnp.repeat(jnp.arange(sequence_length, dtype=jnp.int32), TOPK)
    slot_token = jnp.zeros((buffer_size,), jnp.int32).at[slot_rows].set(token_ids)
    filled = jnp.zeros((buffer_size,), jnp.float32).at[slot_rows].set(1.0)
    expert_in = (normed_moe[slot_token] * filled[:, None]).reshape(EXPERTS, N_TENSOR * CAP, MODEL_WIDTH)
    expert_pre = low_back(jnp.einsum('erd,ecdf->ecrf', expert_in, w_expert_in, precision=highest))
    expert_act = low(jax.nn.silu(expert_pre[:, 0]) * expert_pre[:, 1])
    expert_out = low_back(jnp.einsum('erf,edf->erd', expert_act, w_expert_out, precision=highest)).reshape(-1, MODEL_WIDTH)
    picked = expert_out[slot_rows].reshape(sequence_length, TOPK, MODEL_WIDTH)
    routed = lax.optimization_barrier(jnp.sum(gate_weights[:, :, None] * picked, axis=1))
    branch = low_back(shared_out + routed)
    return (hidden + branch) * valid

def reference(block_input, teacher, lengths, routes, gain_attn, w_query, key_value_weight, w_out, gain_moe, w_router, w_shared_in, w_shared_out, w_expert_in, w_expert_out):
    float_params = tuple((param.astype(jnp.float32) for param in (gain_attn, w_query, key_value_weight, w_out, gain_moe, w_router, w_shared_in, w_shared_out, w_expert_in, w_expert_out)))
    inputs_all = block_input.astype(jnp.float32).reshape(N_DP, SEQ, MODEL_WIDTH)
    route_seq = routes.reshape(N_DP, SEQ, TOPK)

    def forward(inputs_f, *params):

        def one_sequence(packed):
            x_seq, length, route_rows = packed
            return sequence_block(x_seq, length, route_rows, *params)
        return lax.map(jax.checkpoint(one_sequence), (inputs_f, lengths, route_seq))
    result, pullback = jax.vjp(forward, inputs_all, *float_params)
    valid = (jnp.arange(SEQ, dtype=jnp.int32)[None, :] < lengths[:, None]).astype(jnp.float32)[..., None]
    residual_error = (result - teacher.astype(jnp.float32).reshape(N_DP, SEQ, MODEL_WIDTH)) * valid
    valid_count = jnp.sum(lengths).astype(jnp.float32)
    loss = 0.5 * jnp.sum(residual_error * residual_error) / (valid_count * MODEL_WIDTH)
    gradients = pullback(residual_error)
    return (result.reshape(TOKENS, MODEL_WIDTH).astype(jnp.bfloat16), loss, gradients[0].reshape(TOKENS, MODEL_WIDTH), gradients[1], gradients[2], gradients[3], gradients[4], gradients[5], gradients[6], gradients[7], gradients[8], gradients[9], gradients[10])
```

```python
import jax
import jax.numpy as jnp
from jax import lax
from jax.sharding import PartitionSpec as P

HEAD_SIZE = 128
TOPK = 6

norm_eps = 1e-05
masked_score = -1e30
bf16 = jnp.bfloat16
f32 = jnp.float32


def product(left_side, right_side):
    return jnp.dot(left_side, right_side, preferred_element_type=f32)


def product_transposed(left_side, right_side):
    return lax.dot_general(
        left_side, right_side, (((1,), (1,)), ((), ())), preferred_element_type=f32
    )


def product_left(left_side, right_side):
    return lax.dot_general(
        left_side, right_side, (((0,), (0,)), ((), ())), preferred_element_type=f32
    )


def contract(spec, *operands):
    return jnp.einsum(spec, *operands, preferred_element_type=f32)


def normalize_rows(values, gain):
    row_scale = lax.rsqrt(jnp.mean(values * values, axis=-1, keepdims=True) + norm_eps)
    return ((values * row_scale * gain).astype(bf16), row_scale)


def normalize_back(values, row_scale, gain, grad_normed):
    scaled = grad_normed * gain
    inner_mean = jnp.mean(scaled * values, axis=-1, keepdims=True)
    grad_values = row_scale * (scaled - values * row_scale * row_scale * inner_mean)
    grad_gain = jnp.sum(grad_normed * values * row_scale, axis=0)
    return (grad_values, grad_gain)


def swish_back(pre_gate, pre_up, grad_act):
    logistic = jax.nn.sigmoid(pre_gate)
    grad_gate = grad_act * pre_up * logistic * (1.0 + pre_gate * (1.0 - logistic))
    grad_up = grad_act * pre_gate * logistic
    return grad_gate.astype(bf16), grad_up.astype(bf16)


def subset_masks(bits):
    masks = [0]
    for bit in bits:
        masks = masks + [mask | (1 << bit) for mask in masks]
    return masks


class Layout:
    def __init__(self):
        self.dp = lax.axis_size("dp")
        self.tp = lax.axis_size("tensor")
        self.place = lax.axis_index("dp")
        self.core = lax.axis_index("tensor")
        bits = self.dp.bit_length() - 1
        self.w_bits = [bit for bit in (1, 3) if bit < bits]
        self.g_bits = [bit for bit in range(bits) if bit not in self.w_bits]
        self.w_masks = subset_masks(self.w_bits)
        self.g_masks = subset_masks(self.g_bits)
        self.steps = [(bit, bit) for bit in range(bits - 1, 1, -1)] + [(1, 0), (0, 1)]

    def shift(self, values, mask):
        return lax.ppermute(values, "dp", [(i, i ^ mask) for i in range(self.dp)])

    def shift_core(self, values, mask):
        return lax.ppermute(values, "tensor", [(i, i ^ mask) for i in range(self.tp)])

    def shift_step(self, values, step):
        even, odd = step
        pairs = []
        for i in range(self.dp):
            for c in range(self.tp):
                target = i ^ (1 << (odd if c % 2 else even))
                pairs.append((i * self.tp + c, target * self.tp + c))
        return lax.ppermute(values, ("dp", "tensor"), pairs)

    def step_bit(self, step):
        even, odd = step
        return even if even == odd else jnp.where(self.core % 2 == 1, odd, even)

    def gather_dp(self, shard):
        held = shard[None]
        for step in self.steps:
            held = jnp.concatenate([held, self.shift_step(held, step)], axis=0)
        apart = self.place ^ jnp.arange(self.dp)
        at = sum(((apart >> self.step_bit(step)) & 1) << k for k, step in enumerate(self.steps))
        return held[at].reshape((-1,) + shard.shape[1:])

    def scatter_dp(self, whole):
        blocks = whole.astype(bf16).reshape((self.dp, -1) + whole.shape[1:])
        rel = jnp.arange(self.dp)
        apart = sum(((rel >> k) & 1) << self.step_bit(step) for k, step in enumerate(self.steps))
        at = self.place ^ apart
        half = self.dp // 2
        keep, send = blocks[at[:half]].astype(f32), blocks[at[half:]]
        for k in range(len(self.steps) - 1, -1, -1):
            total = keep + self.shift_step(send, self.steps[k]).astype(f32)
            half = half // 2
            if k > 0:
                keep, send = total[:half], total[half:].astype(bf16)
        return total[0]

    def gather_g(self, values):
        return [values] + [self.shift(values, mask) for mask in self.g_masks[1:]]

    def gather_w(self, values):
        held = [values]
        for bit in reversed(self.w_bits):
            held = held + [self.shift(v, 1 << bit) for v in held]
        order = subset_masks(list(reversed(self.w_bits)))
        return [held[order.index(mask)] for mask in self.w_masks]

    def scatter_w(self, blocks):
        order = subset_masks(list(reversed(self.w_bits)))
        held = [blocks[self.w_masks.index(mask)] for mask in order]
        for bit in self.w_bits:
            half = len(held) // 2
            held = [
                keep.astype(f32) + self.shift(send.astype(bf16), 1 << bit).astype(f32)
                for keep, send in zip(held[:half], held[half:])
            ]
        return held[0]

    def gather_core(self, values):
        return [values] + [self.shift_core(values, k) for k in range(1, self.tp)]

    def scatter_core(self, blocks):
        total = blocks[0].astype(f32)
        for k in range(1, self.tp):
            total = total + self.shift_core(blocks[k].astype(bf16), k).astype(f32)
        return total

    def sum_all(self, values):
        for bit in range(self.dp.bit_length() - 1):
            values = values + self.shift(values, 1 << bit)
        for bit in range(self.tp.bit_length() - 1):
            values = values + self.shift_core(values, 1 << bit)
        return values

    def chunk(self, mask):
        place = self.place ^ mask
        return sum(((place >> bit) & 1) << k for k, bit in enumerate(self.g_bits))

    def rows_order(self):
        apart = self.place ^ jnp.arange(self.dp)
        g = sum(((apart >> bit) & 1) << k for k, bit in enumerate(self.g_bits))
        w = sum(((apart >> bit) & 1) << k for k, bit in enumerate(self.w_bits))
        return g * len(self.w_masks) + w

    def rows_apart(self):
        masks = jnp.array([g | w for g in self.g_masks for w in self.w_masks], jnp.int32)
        return self.place ^ masks


def gather_shared(lay, shared_in, shared_out):
    part = shared_out.shape[1] // len(lay.g_masks)
    rows = shared_out.shape[0]
    stacked = jnp.concatenate([shared_in, shared_out[None]], axis=0)

    def piece(mask):
        return lax.dynamic_slice_in_dim(stacked, lay.chunk(mask) * part, part, 2)

    arrived = jnp.stack([piece(0)] + [lay.shift(piece(m), m) for m in lay.g_masks[1:]])
    everyone = jnp.stack(lay.gather_w(arrived), axis=1)
    natural = everyone.reshape((lay.dp, 3, rows, part))[lay.rows_order()]
    own = natural.transpose(1, 0, 2, 3).reshape(3, lay.dp * rows, part)
    return jnp.concatenate(lay.gather_core(own), axis=2)


def scatter_shared(lay, grads):
    part = grads.shape[2] // lay.tp
    rows = grads.shape[1] // lay.dp
    own = lay.scatter_core([grads[:, :, k * part : (k + 1) * part] for k in range(lay.tp)])
    natural = own.astype(bf16).reshape(3, lay.dp, rows, part).transpose(1, 0, 2, 3)
    blocks = natural[lay.rows_apart()].reshape(len(lay.g_masks), len(lay.w_masks), 3, rows, part)
    summed = lay.scatter_w([blocks[:, k] for k in range(len(lay.w_masks))])
    out = jnp.zeros((3, rows, part * len(lay.g_masks)), f32)
    for k, mask in enumerate(lay.g_masks):
        got = summed[k] if k == 0 else lay.shift(summed[k].astype(bf16), mask).astype(f32)
        out = lax.dynamic_update_slice_in_dim(out, got, lay.chunk(mask) * part, 2)
    return out


def on_device(
    block_input,
    teacher,
    lengths,
    routes,
    gain_attn,
    w_query,
    key_value_weight,
    w_out,
    gain_moe,
    w_router,
    w_shared_in,
    w_shared_out,
    w_expert_in,
    w_expert_out,
):
    lay = Layout()
    own_rows, width = block_input.shape
    tp, dp = lay.tp, lay.dp
    sequence_length = own_rows * tp
    experts = w_expert_in.shape[0] * dp
    capacity = max(2, own_rows * TOPK * 4 // (3 * experts))
    n_g, n_w = len(lay.g_masks), len(lay.w_masks)
    length = lengths[lay.place]
    slices = jnp.array(range(tp), jnp.int32) ^ lay.core
    positions = (slices[:, None] * own_rows + jnp.arange(own_rows)[None, :]).reshape(-1)
    own_valid = (positions[:own_rows] < length).astype(f32)[:, None]
    head_count = w_query.shape[1] // HEAD_SIZE
    kv_count = key_value_weight.shape[2] // HEAD_SIZE
    head_group = head_count // kv_count
    q_dim, kv_dim = head_count * HEAD_SIZE, kv_count * HEAD_SIZE

    qkv_full = lay.gather_dp(
        jnp.concatenate([w_query, key_value_weight[0], key_value_weight[1]], axis=1)
    )
    out_full = lay.gather_dp(w_out)
    router_full = lax.all_gather(w_router, "dp", axis=0, tiled=True)
    shared_full = gather_shared(lay, w_shared_in, w_shared_out)
    shared_in_full, shared_out_full = shared_full[:2], shared_full[2]
    expert_own = jnp.concatenate([w_expert_in[0], w_expert_out], axis=0)
    expert_parts = lay.gather_core(jnp.stack(lay.gather_w(expert_own)))
    expert_whole = jnp.concatenate(expert_parts, axis=3)
    expert_in_whole, expert_out_whole = expert_whole[:, :2], expert_whole[:, 2]

    inputs_all = jnp.concatenate(lay.gather_core(block_input), axis=0).astype(f32)
    normed_all, scale_all = normalize_rows(inputs_all, gain_attn)
    residual, scale_attn = inputs_all[:own_rows], scale_all[:own_rows]
    projected = product(normed_all, qkv_full).astype(bf16)
    queries = projected[:, :q_dim].reshape(sequence_length, kv_count, head_group, HEAD_SIZE)
    key_row_table = projected[:, q_dim : q_dim + kv_dim].reshape(
        sequence_length, kv_count, HEAD_SIZE
    )
    value_row_table = projected[:, q_dim + kv_dim :].reshape(sequence_length, kv_count, HEAD_SIZE)
    allowed = (positions[None, :] <= positions[:, None]) & (positions[None, :] < length)
    scores = contract("qvgd,kvd->vgqk", queries, key_row_table) * HEAD_SIZE ** (-0.5)
    scores = jnp.where(allowed, scores, masked_score)
    row_max = jnp.max(scores, axis=-1, keepdims=True)
    exponent_terms = jnp.exp(scores - row_max)
    row_sum = jnp.sum(exponent_terms, axis=-1, keepdims=True)
    probs_full = exponent_terms / row_sum
    probs_low = probs_full.astype(bf16)
    mixed_heads = (
        contract("vgqk,kvd->qvgd", probs_low, value_row_table)
        .astype(bf16)
        .reshape(sequence_length, q_dim)
    )

    def by_core(rows):
        return [rows[k * own_rows : (k + 1) * own_rows] for k in range(tp)]

    hidden = residual + lay.scatter_core(by_core(product_transposed(mixed_heads, out_full)))
    moe_own, scale_moe = normalize_rows(hidden, gain_moe)

    own_routes = lax.dynamic_slice_in_dim(routes, lay.core * own_rows, own_rows, 0)
    group_routes = jnp.stack(lay.gather_g(own_routes))
    expert_ids = jnp.arange(experts, dtype=jnp.int32)
    member = jnp.any(group_routes[:, :, :, None] == expert_ids, axis=2)
    held_ids = lay.place ^ jnp.array(lay.w_masks, jnp.int32)
    held_member = jnp.any(group_routes[:, :, :, None] == held_ids, axis=2).astype(bf16)
    before = jnp.tril(jnp.ones((own_rows, own_rows), bf16), -1)
    position = contract("ut,gtj->guj", before, held_member)
    position = jnp.where(held_member > 0, position, -1.0)
    dispatch = (
        position.transpose(0, 2, 1)[:, :, None, :] == jnp.arange(capacity, dtype=f32)[:, None]
    ).astype(bf16)

    moe_all = jnp.stack(lay.gather_g(moe_own))
    logits = contract("gtd,de->gte", moe_all, router_full)
    shown = jnp.where(member, logits, masked_score)
    gate_terms = jnp.exp(shown - jnp.max(shown, axis=-1, keepdims=True))
    gates = gate_terms / jnp.sum(gate_terms, axis=-1, keepdims=True)
    held_gates = jnp.sum(gates[:, :, None, :] * (expert_ids == held_ids[:, None]), axis=-1)
    slot_gate = jnp.sum(dispatch.astype(f32) * held_gates.transpose(0, 2, 1)[:, :, None, :], axis=-1)
    slot_gate = slot_gate.transpose(1, 0, 2).reshape(n_w, n_g * capacity, 1)
    group_rows = moe_all.reshape(n_g * own_rows, width)
    shared_pre = contract("td,cdf->ctf", group_rows, shared_in_full)
    shared_act = (jax.nn.silu(shared_pre[0]) * shared_pre[1]).astype(bf16)
    work_rows = (
        contract("gjct,gtd->jgcd", dispatch, moe_all)
        .astype(bf16)
        .reshape(n_w, n_g * capacity, width)
    )
    pre_acts = contract("jrd,jcdf->jcrf", work_rows, expert_in_whole)
    activated = jax.nn.silu(pre_acts[:, 0]) * pre_acts[:, 1]
    act_low = activated.astype(bf16)
    produced = (contract("jrf,jdf->jrd", act_low, expert_out_whole) * slot_gate).astype(bf16)
    combined = contract(
        "gjct,jgcd->gtd", dispatch, produced.reshape(n_w, n_g, capacity, width)
    ) + product_transposed(shared_act, shared_out_full).reshape(n_g, own_rows, width)

    def scatter_g(parts):
        total = parts[0].astype(f32)
        for k in range(1, n_g):
            total = total + lay.shift(parts[k].astype(bf16), lay.g_masks[k]).astype(f32)
        return total

    out_rows = (hidden + scatter_g([combined[k] for k in range(n_g)])) * own_valid
    residual_error = (out_rows - teacher.astype(f32)) * own_valid
    loss_part = 0.5 * jnp.sum(residual_error * residual_error)

    grad_all = jnp.stack(lay.gather_g(residual_error.astype(bf16)))
    grad_rows = (
        contract("gjct,gtd->jgcd", dispatch, grad_all)
        .astype(bf16)
        .reshape(n_w, n_g * capacity, width)
    )
    back_act = contract("jrd,jdf->jrf", grad_rows, expert_out_whole)
    slot_grad_gate = jnp.sum(back_act * act_low.astype(f32), axis=-1)
    grad_wout = contract("jrd,jrf->jdf", grad_rows, (activated * slot_gate).astype(bf16))
    grad_gate_pre, grad_up_pre = swish_back(pre_acts[:, 0], pre_acts[:, 1], back_act * slot_gate)
    grad_pre = jnp.stack([grad_gate_pre, grad_up_pre], axis=1)
    grad_win = contract("jrd,jcrf->jcdf", work_rows, grad_pre)
    grad_inputs = contract("jcrf,jcdf->jrd", grad_pre, expert_in_whole).astype(bf16)
    group_grad = grad_all.reshape(n_g * own_rows, width)
    grad_shared_act = product(group_grad, shared_out_full)
    grad_shared_out = product_left(group_grad, shared_act)
    grad_shared_pre = jnp.stack(swish_back(shared_pre[0], shared_pre[1], grad_shared_act))
    grad_shared_in = contract("td,ctf->cdf", group_rows, grad_shared_pre)
    grad_combined = contract(
        "gjct,jgcd->gtd", dispatch, grad_inputs.reshape(n_w, n_g, capacity, width)
    ) + contract("ctf,cdf->td", grad_shared_pre, shared_in_full).reshape(n_g, own_rows, width)
    held_grad_gates = jnp.sum(
        dispatch.astype(f32) * slot_grad_gate.reshape(n_w, n_g, capacity).transpose(1, 0, 2)[..., None],
        axis=2,
    )
    spread = (expert_ids[None, :] == held_ids[:, None]).astype(f32)
    grad_gates_part = jnp.sum(held_grad_gates[..., None] * spread[None, :, None, :], axis=1)
    high = grad_gates_part.astype(bf16)
    low = (grad_gates_part - high.astype(f32)).astype(bf16)
    pad = -(2 * experts) % 128
    payload = jnp.concatenate(
        [grad_combined.astype(bf16), high, low, jnp.zeros((n_g, own_rows, pad), bf16)], axis=-1
    )
    returned = scatter_g([payload[k] for k in range(n_g)])
    grad_gates = returned[:, width : width + experts] + returned[:, width + experts : width + 2 * experts]
    own_gates = gates[0]
    grad_logits = (
        own_gates * (grad_gates - jnp.sum(own_gates * grad_gates, axis=-1, keepdims=True))
    ).astype(bf16)
    grad_router_part = product_left(moe_own, grad_logits)
    grad_normed_own = returned[:, :width] + product_transposed(grad_logits, router_full)

    grad_expert = jnp.concatenate([grad_win, grad_wout[:, None]], axis=1)
    part = grad_expert.shape[3] // tp
    grad_expert = lay.scatter_core(
        [grad_expert[..., k * part : (k + 1) * part] for k in range(tp)]
    )
    grad_expert = lay.scatter_w([grad_expert[k] for k in range(n_w)])
    grad_w_expert_in, grad_w_expert_out = grad_expert[None, :2], grad_expert[2:3]
    grad_shared = scatter_shared(lay, jnp.concatenate([grad_shared_in, grad_shared_out[None]]))

    grad_from_moe, grad_gain_moe_part = normalize_back(hidden, scale_moe, gain_moe, grad_normed_own)
    grad_hidden = residual_error + grad_from_moe
    grad_attn = jnp.concatenate(lay.gather_core(grad_hidden.astype(bf16)), axis=0)
    grad_w_out = lay.scatter_dp(product_left(grad_attn, mixed_heads))
    grad_mixed = (
        product(grad_attn, out_full)
        .astype(bf16)
        .reshape(sequence_length, kv_count, head_group, HEAD_SIZE)
    )
    grad_values = contract("vgqk,qvgd->kvd", probs_low, grad_mixed)
    grad_probs = contract("qvgd,kvd->vgqk", grad_mixed, value_row_table)
    delta_sum = jnp.sum(probs_full * grad_probs, axis=-1, keepdims=True)
    grad_scores = (probs_full * (grad_probs - delta_sum)).astype(bf16)
    grad_queries = contract("vgqk,kvd->qvgd", grad_scores, key_row_table) * HEAD_SIZE ** (-0.5)
    grad_keys = contract("vgqk,qvgd->kvd", grad_scores, queries) * HEAD_SIZE ** (-0.5)
    grad_projected = jnp.concatenate(
        [
            grad_queries.astype(bf16).reshape(sequence_length, q_dim),
            grad_keys.astype(bf16).reshape(sequence_length, kv_dim),
            grad_values.astype(bf16).reshape(sequence_length, kv_dim),
        ],
        axis=1,
    )
    grad_qkv = lay.scatter_dp(product_left(normed_all, grad_projected))
    grad_normed_attn = lay.scatter_core(by_core(product_transposed(grad_projected, qkv_full)))
    grad_from_attn, grad_gain_attn_part = normalize_back(
        residual, scale_attn, gain_attn, grad_normed_attn
    )
    input_grad = grad_hidden + grad_from_attn
    grad_w_kv = jnp.stack(
        [grad_qkv[:, q_dim : q_dim + kv_dim], grad_qkv[:, q_dim + kv_dim :]], axis=0
    )
    grad_w_router = lax.psum_scatter(
        lay.scatter_core([grad_router_part, grad_router_part]) if tp == 2 else lax.psum(grad_router_part, "tensor"),
        "dp",
        scatter_dimension=0,
        tiled=True,
    )
    small = jnp.stack(
        [grad_gain_attn_part, grad_gain_moe_part, jnp.full((width,), loss_part, f32)], axis=0
    )
    small = lay.sum_all(small)
    loss = small[2, 0] / (jnp.sum(lengths).astype(f32) * width)
    return (
        out_rows.astype(bf16),
        loss,
        input_grad,
        small[0],
        grad_qkv[:, :q_dim],
        grad_w_kv,
        grad_w_out,
        small[1],
        grad_w_router,
        grad_shared[:2],
        grad_shared[2],
        grad_w_expert_in,
        grad_w_expert_out,
    )


def solution(mesh):
    rows, weights = P(("dp", "tensor"), None), P("dp", "tensor")
    stacked = P(None, "dp", "tensor")
    expert_in, expert_out = P("dp", None, None, "tensor"), P("dp", None, "tensor")
    return jax.shard_map(
        on_device,
        mesh=mesh,
        in_specs=(
            rows,
            rows,
            P(),
            P("dp", None),
            P(),
            weights,
            stacked,
            weights,
            P(),
            P("dp", None),
            stacked,
            weights,
            expert_in,
            expert_out,
        ),
        out_specs=(
            rows,
            P(),
            rows,
            P(),
            weights,
            stacked,
            weights,
            P(),
            P("dp", None),
            stacked,
            weights,
            expert_in,
            expert_out,
        ),
        check_vma=False,
    )
```

```python
import jax
import jax.numpy as jnp
from jax import lax
from jax.experimental import pallas as pl
from jax.experimental.pallas import tpu as pltpu
from jax.sharding import PartitionSpec as P

HEAD_SIZE = 128
TOPK = 6

norm_eps = 1e-05
masked_score = -1e30
TAIL = 16
bf16 = jnp.bfloat16
f32 = jnp.float32


def product(left_side, right_side):
    return jnp.dot(left_side, right_side, preferred_element_type=f32)


def product_transposed(left_side, right_side):
    return lax.dot_general(
        left_side, right_side, (((1,), (1,)), ((), ())), preferred_element_type=f32
    )


def product_left(left_side, right_side):
    return lax.dot_general(
        left_side, right_side, (((0,), (0,)), ((), ())), preferred_element_type=f32
    )


def contract(spec, *operands):
    return jnp.einsum(spec, *operands, preferred_element_type=f32)


def normalize_rows(values, gain):
    row_scale = lax.rsqrt(jnp.mean(values * values, axis=-1, keepdims=True) + norm_eps)
    return ((values * row_scale * gain).astype(bf16), row_scale)


def normalize_back(values, row_scale, gain, grad_normed):
    scaled = grad_normed * gain
    inner_mean = jnp.mean(scaled * values, axis=-1, keepdims=True)
    grad_values = row_scale * (scaled - values * row_scale * row_scale * inner_mean)
    grad_gain = jnp.sum(grad_normed * values * row_scale, axis=0)
    return (grad_values, grad_gain)


def swish_back(pre_gate, pre_up, grad_act):
    logistic = jax.nn.sigmoid(pre_gate)
    grad_gate = grad_act * pre_up * logistic * (1.0 + pre_gate * (1.0 - logistic))
    grad_up = grad_act * pre_gate * logistic
    return grad_gate.astype(bf16), grad_up.astype(bf16)


def subset_masks(bits):
    masks = [0]
    for bit in bits:
        masks = masks + [mask | (1 << bit) for mask in masks]
    return masks


def behind(values, *others):
    return lax.optimization_barrier((values,) + others)[0]


class Tree:
    def __init__(self, lay, shard):
        self.lay, self.halves, self.marks = lay, (shard[None],), []

    def step(self, *others):
        held = jnp.concatenate(self.halves, axis=0)
        if others:
            held = behind(held, *others)
        self.marks.append(self.lay.shift_step(held, self.lay.steps[len(self.marks)]))
        self.halves = (held, self.marks[-1])
        return self.marks[-1]


class Sum:
    def __init__(self, lay, halves):
        self.lay, (self.keep, self.send), self.marks = lay, halves, []

    def step(self, *others):
        got = self.lay.shift(self.send, 1 << self.lay.back_bits[-1 - len(self.marks)])
        if others:
            got = behind(got, *others)
        self.marks.append(got)
        self.total = self.keep.astype(f32) + got.astype(f32)
        half = self.total.shape[0] // 2
        self.keep, self.send = self.total[:half], self.total[half:].astype(bf16)
        return got


class Layout:
    def __init__(self):
        self.dp = lax.axis_size("dp")
        self.tp = lax.axis_size("tensor")
        self.place = lax.axis_index("dp")
        self.core = lax.axis_index("tensor")
        bits = self.dp.bit_length() - 1
        self.w_bits = [bit for bit in (1, 3) if bit < bits]
        self.g_bits = [bit for bit in range(bits) if bit not in self.w_bits]
        self.w_masks = subset_masks(self.w_bits)
        self.g_masks = subset_masks(self.g_bits)
        self.steps = [(bit, bit) for bit in range(bits - 1, 1, -1)] + [(1, 0), (0, 1)]
        self.back_bits = list(range(bits - 1, -1, -1))

    def shift(self, values, mask):
        return lax.ppermute(values, "dp", [(i, i ^ mask) for i in range(self.dp)])

    def w_groups(self):
        groups = []
        for i in range(self.dp):
            if all(i & mask == 0 for mask in self.w_masks):
                places = sorted(i ^ mask for mask in self.w_masks)
                groups.append([place * self.tp + c for place in places for c in range(self.tp)])
        return groups

    def w_spots(self):
        bits = [(self.place >> bit) & 1 for bit in self.w_bits]
        rows = []
        for k in range(len(self.w_masks)):
            spot = sum((bit ^ ((k >> n) & 1)) << n for n, bit in enumerate(bits))
            rows.append(jnp.stack([spot * self.tp + (self.core ^ c) for c in range(self.tp)]))
        return jnp.stack(rows).astype(jnp.int32)

    def shift_core(self, values, mask):
        return lax.ppermute(values, "tensor", [(i, i ^ mask) for i in range(self.tp)])

    def shift_step(self, values, step):
        even, odd = step
        pairs = []
        for i in range(self.dp):
            for c in range(self.tp):
                target = i ^ (1 << (odd if c % 2 else even))
                pairs.append((i * self.tp + c, target * self.tp + c))
        return lax.ppermute(values, ("dp", "tensor"), pairs)

    def step_bit(self, step):
        even, odd = step
        return even if even == odd else jnp.where(self.core % 2 == 1, odd, even)

    def gather_order(self):
        apart = self.place ^ jnp.arange(self.dp)
        return sum(((apart >> self.step_bit(step)) & 1) << k for k, step in enumerate(self.steps))

    def scatter_order(self):
        apart = self.place ^ jnp.arange(self.dp)
        return sum(((apart >> bit) & 1) << k for k, bit in enumerate(self.back_bits))

    def in_order(self, halves):
        whole = jnp.concatenate(halves, axis=0)[self.gather_order()]
        return whole.reshape((-1,) + whole.shape[2:])

    def in_halves(self, whole):
        blocks = whole.astype(bf16).reshape((self.dp, -1) + whole.shape[1:])
        rel = jnp.arange(self.dp)
        apart = sum(((rel >> k) & 1) << bit for k, bit in enumerate(self.back_bits))
        at = self.place ^ apart
        return blocks[at[: self.dp // 2]], blocks[at[self.dp // 2 :]]

    def gather_g(self, values):
        return [values] + [self.shift(values, mask) for mask in self.g_masks[1:]]

    def scatter_w(self, blocks, after):
        near, far = (1 << bit for bit in self.w_bits)
        both = jnp.stack([blocks[3], blocks[1]]).astype(bf16)
        far_one, own = behind(self.shift(both, near), after)
        far_one = self.shift((blocks[2].astype(f32) + far_one.astype(f32)).astype(bf16), far)
        return blocks[0].astype(f32) + own.astype(f32) + far_one.astype(f32)

    def gather_core(self, values):
        return [values] + [self.shift_core(values, k) for k in range(1, self.tp)]

    def scatter_core(self, blocks):
        total = blocks[0].astype(f32)
        for k in range(1, self.tp):
            total = total + self.shift_core(blocks[k].astype(bf16), k).astype(f32)
        return total

    def sum_all(self, values, marks):
        for bit, mark in enumerate(marks):
            values = behind(values, mark)
            values = values + self.shift(values, 1 << bit)
        for bit in range(self.tp.bit_length() - 1):
            values = values + self.shift_core(values, 1 << bit)
        return values

    def chunk(self, mask):
        place = self.place ^ mask
        return sum(((place >> bit) & 1) << k for k, bit in enumerate(self.g_bits))

    def rows_order(self):
        apart = self.place ^ jnp.arange(self.dp)
        g = sum(((apart >> bit) & 1) << k for k, bit in enumerate(self.g_bits))
        w = sum(((apart >> bit) & 1) << k for k, bit in enumerate(self.w_bits))
        return g * len(self.w_masks) + w

    def rows_apart(self):
        masks = jnp.array([g | w for g in self.g_masks for w in self.w_masks], jnp.int32)
        return self.place ^ masks


def slots_of(position, capacity):
    slots = jnp.arange(capacity, dtype=f32)[:, None]
    return (position[:, :, None, :] == slots).astype(bf16)


def experts_forward_plain(position, gate, spots, capacity, tokens, shares, init):
    (held, groups, rows), width = position.shape, tokens.shape[1]
    taken = slots_of(position, capacity)
    work = contract("jgct,gtd->jgcd", taken, tokens.reshape(groups, rows, width)).astype(bf16)
    work = work.reshape(held, groups * capacity, width)
    scale = jnp.sum(taken.astype(f32) * gate[:, :, None, :], axis=-1).reshape(held, -1, 1)
    pre, made = [], 0.0
    for c in range(spots.shape[1]):
        weight = shares[spots[:, c]]
        pre.append(contract("jrd,jsdf->jsrf", work, weight[:, :2]))
        act = (jax.nn.silu(pre[-1][:, 0]) * pre[-1][:, 1]).astype(bf16)
        made = made + contract("jrf,jdf->jrd", act, weight[:, 2])
    made = (made * scale).astype(bf16).reshape(held, groups, capacity, width)
    total = init.reshape(groups, rows, width) + contract("jgct,jgcd->gtd", taken, made)
    return total.astype(bf16), work, jnp.stack(pre, axis=1)


def experts_backward_plain(position, gate, spots, capacity, tokens, work, pre, shares, init):
    (held, groups, rows), width = position.shape, tokens.shape[1]
    taken = slots_of(position, capacity)
    grad_rows = contract("jgct,gtd->jgcd", taken, tokens.reshape(groups, rows, width)).astype(bf16)
    grad_rows = grad_rows.reshape(held, groups * capacity, width)
    scale = jnp.sum(taken.astype(f32) * gate[:, :, None, :], axis=-1).reshape(held, -1, 1)
    chosen, made, grads = 0.0, 0.0, jnp.zeros(shares.shape, bf16)
    for c in range(spots.shape[1]):
        weight = shares[spots[:, c]]
        back = contract("jrd,jdf->jrf", grad_rows, weight[:, 2])
        activated = jax.nn.silu(pre[:, c, 0]) * pre[:, c, 1]
        chosen = chosen + jnp.sum(back * activated, axis=-1)
        grad_pre = jnp.stack(swish_back(pre[:, c, 0], pre[:, c, 1], back * scale), axis=1)
        made = made + contract("jsrf,jsdf->jrd", grad_pre, weight[:, :2])
        grad_in = contract("jrd,jsrf->jsdf", work, grad_pre).astype(bf16)
        grad_out = contract("jrd,jrf->jdf", grad_rows, (activated * scale).astype(bf16)).astype(bf16)
        grads = grads.at[spots[:, c]].set(jnp.concatenate([grad_in, grad_out[:, None]], axis=1))
    made = made.astype(bf16).reshape(held, groups, capacity, width)
    total = init.reshape(groups, rows, width) + contract("jgct,jgcd->gtd", taken, made)
    chosen = jnp.sum(taken.astype(f32) * chosen.reshape(held, groups, capacity, 1), axis=2)
    tail = chosen.transpose(1, 0, 2)
    high = tail.astype(bf16).astype(f32)
    tail = jnp.concatenate([high, tail - high], axis=1)
    tail = jnp.pad(tail, ((0, 0), (0, TAIL - tail.shape[1]), (0, width - rows)))
    return jnp.concatenate([total, tail], axis=1).astype(bf16), grads


def dot_rows(left, right):
    return lax.dot_general(left, right, (((0,), (0,)), ((), ())), preferred_element_type=f32)


def slot_matrix(position, capacity):
    slots = lax.broadcasted_iota(jnp.int32, (capacity, position.shape[1]), 0).astype(f32)
    return slots == position


def block_copies(order, whole, halves, sems, inward):
    blocks, rows = halves[0].shape[0], halves[0].shape[1]
    for i in range(2 * blocks):
        part = whole.at[pl.ds(i * rows, rows)]
        for k, half in enumerate(halves):

            @pl.when((order[i] >= k * blocks) & (order[i] < (k + 1) * blocks))
            def _():
                block = half.at[order[i] - k * blocks]
                source, target = (block, part) if inward else (part, block)
                pltpu.make_async_copy(source, target, sems.at[i]).start()


def block_waits(whole, halves, sems, inward):
    blocks, rows = halves[0].shape[0], halves[0].shape[1]
    for i in range(2 * blocks):
        part = whole.at[pl.ds(i * rows, rows)]
        source, target = (halves[0].at[0], part) if inward else (part, halves[0].at[0])
        pltpu.make_async_copy(source, target, sems.at[i]).wait()


def score_mask(core, length, rows):
    row = lax.broadcasted_iota(jnp.int32, (rows, rows), 0)
    col = lax.broadcasted_iota(jnp.int32, (rows, rows), 1)
    first = core * (rows // 2)
    row = jnp.where(row < rows // 2, row + first, row - first)
    col = jnp.where(col < rows // 2, col + first, col - first)
    return (col <= row) & (col < length)


anywhere = pl.BlockSpec(memory_space=pl.ANY)
scalars = pl.BlockSpec(memory_space=pltpu.SMEM)
in_vmem = pl.BlockSpec(memory_space=pltpu.VMEM)
no_cost = pl.CostEstimate(flops=0, transcendentals=0, bytes_accessed=0)
room = pltpu.CompilerParams(vmem_limit_bytes=56 * 1024 * 1024)


def attend(order, spot, own, other, gain, halves, head_count, kv_count):
    rows, width = own.shape
    total, columns = 2 * rows, halves[0].shape[2]
    group = head_count // kv_count

    def kernel(order, spot, own, other, gain, near, far, normed, made, mixed, logs, weight, sems):
        block_copies(order, weight, (near, far), sems, True)
        for k, part in enumerate((own, other)):
            values = part[...].astype(f32)
            scale = lax.rsqrt(jnp.mean(values * values, axis=1, keepdims=True) + norm_eps)
            normed[pl.ds(k * rows, rows), :] = (values * scale * gain[...]).astype(bf16)
        block_waits(weight, (near, far), sems, True)
        made[...] = product(normed[...], weight[...]).astype(bf16)
        allowed = score_mask(spot[0], spot[1], total)
        for h in range(head_count):
            key = pl.ds((head_count + h // group) * HEAD_SIZE, HEAD_SIZE)
            value = pl.ds((head_count + kv_count + h // group) * HEAD_SIZE, HEAD_SIZE)
            at = pl.ds(h * HEAD_SIZE, HEAD_SIZE)
            scores = product_transposed(made[:, at], made[:, key]) * HEAD_SIZE ** (-0.5)
            scores = jnp.where(allowed, scores, masked_score)
            most = jnp.max(scores, axis=1, keepdims=True)
            terms = jnp.exp(scores - most)
            together = jnp.sum(terms, axis=1, keepdims=True)
            probs = (terms * (1.0 / together)).astype(bf16)
            mixed[:, at] = product(probs, made[:, value]).astype(bf16)
            logs[h] = most + jnp.log(together)

    return pl.pallas_call(
        kernel,
        in_specs=[scalars, scalars, in_vmem, in_vmem, in_vmem, anywhere, anywhere],
        out_specs=[in_vmem] * 4,
        out_shape=[
            jax.ShapeDtypeStruct((total, width), bf16),
            jax.ShapeDtypeStruct((total, columns), bf16),
            jax.ShapeDtypeStruct((total, head_count * HEAD_SIZE), bf16),
            jax.ShapeDtypeStruct((head_count, total, 1), f32),
        ],
        scratch_shapes=[
            pltpu.VMEM((width, columns), bf16),
            pltpu.SemaphoreType.DMA((2 * halves[0].shape[0],)),
        ],
        compiler_params=room,
        cost_estimate=no_cost,
    )(order, spot, own, other, gain[None], *halves)


def project_out(order, mixed, halves):
    total, columns = mixed.shape
    width = 2 * halves[0].shape[0] * halves[0].shape[1]
    rows = total // 2

    def kernel(order, mixed, near, far, own, other, weight, sems):
        block_copies(order, weight, (near, far), sems, True)
        block_waits(weight, (near, far), sems, True)
        other[...] = product_transposed(mixed[pl.ds(rows, rows), :], weight[:, :columns]).astype(bf16)
        own[...] = product_transposed(mixed[pl.ds(0, rows), :], weight[:, :columns])

    return pl.pallas_call(
        kernel,
        in_specs=[scalars, in_vmem, anywhere, anywhere],
        out_specs=[in_vmem] * 3,
        out_shape=[
            jax.ShapeDtypeStruct((rows, width), f32),
            jax.ShapeDtypeStruct((rows, width), bf16),
            jax.ShapeDtypeStruct((width, halves[0].shape[2]), bf16),
        ],
        scratch_shapes=[pltpu.SemaphoreType.DMA((2 * halves[0].shape[0],))],
        compiler_params=room,
        cost_estimate=no_cost,
    )(order, mixed, *halves)


def half_shapes(places, width, columns):
    block = jax.ShapeDtypeStruct((places // 2, width // places, columns), bf16)
    return [block, block]


def project_out_back(order, own, other, weight, mixed, router):
    total, columns = mixed.shape
    rows, width = own.shape
    places = order.shape[0]

    def kernel(order, own, other, weight, mixed, router, grad_mixed, near, far, grads, both, sems):
        both[pl.ds(0, rows), :] = own[...]
        both[pl.ds(rows, rows), :] = other[...]
        grads[:, :columns] = dot_rows(both[...], mixed[...]).astype(bf16)
        grads[:, columns:] = router[...]
        block_copies(order, grads, (near, far), sems, False)
        grad_mixed[...] = product(both[...], weight[:, :columns]).astype(bf16)
        block_waits(grads, (near, far), sems, False)

    return pl.pallas_call(
        kernel,
        in_specs=[scalars] + [in_vmem] * 5,
        out_specs=[in_vmem, anywhere, anywhere],
        out_shape=[jax.ShapeDtypeStruct((total, columns), bf16)]
        + half_shapes(places, width, weight.shape[1]),
        scratch_shapes=[
            pltpu.VMEM(weight.shape, bf16),
            pltpu.VMEM((total, width), bf16),
            pltpu.SemaphoreType.DMA((places,)),
        ],
        compiler_params=room,
        cost_estimate=no_cost,
    )(order, own, other, weight, mixed, router)


def attend_back(order, spot, grad_mixed, normed, made, logs, head_count, kv_count):
    total, width = normed.shape
    columns, group = made.shape[1], head_count // kv_count
    places = order.shape[0]

    def kernel(order, spot, grad_mixed, normed, made, logs, grad_made, near, far, grads, sems):
        allowed = score_mask(spot[0], spot[1], total)
        for v in range(kv_count):
            key = pl.ds((head_count + v) * HEAD_SIZE, HEAD_SIZE)
            value = pl.ds((head_count + kv_count + v) * HEAD_SIZE, HEAD_SIZE)
            grad_key, grad_value = 0.0, 0.0
            for h in range(v * group, (v + 1) * group):
                at = pl.ds(h * HEAD_SIZE, HEAD_SIZE)
                scores = product_transposed(made[:, at], made[:, key]) * HEAD_SIZE ** (-0.5)
                probs = jnp.where(allowed, jnp.exp(scores - logs[h]), 0.0)
                grad_value = grad_value + dot_rows(probs.astype(bf16), grad_mixed[:, at])
                grad_probs = product_transposed(grad_mixed[:, at], made[:, value])
                delta = jnp.sum(probs * grad_probs, axis=1, keepdims=True)
                grad_scores = (probs * (grad_probs - delta)).astype(bf16)
                grad_query = product(grad_scores, made[:, key]) * HEAD_SIZE ** (-0.5)
                grad_made[:, at] = grad_query.astype(bf16)
                grad_key = grad_key + dot_rows(grad_scores, made[:, at]) * HEAD_SIZE ** (-0.5)
            grad_made[:, key] = grad_key.astype(bf16)
            grad_made[:, value] = grad_value.astype(bf16)
        grads[...] = dot_rows(normed[...], grad_made[...]).astype(bf16)
        block_copies(order, grads, (near, far), sems, False)
        block_waits(grads, (near, far), sems, False)

    return pl.pallas_call(
        kernel,
        in_specs=[scalars, scalars] + [in_vmem] * 4,
        out_specs=[in_vmem, anywhere, anywhere],
        out_shape=[jax.ShapeDtypeStruct((total, columns), bf16)]
        + half_shapes(places, width, columns),
        scratch_shapes=[
            pltpu.VMEM((width, columns), bf16),
            pltpu.SemaphoreType.DMA((places,)),
        ],
        compiler_params=room,
        cost_estimate=no_cost,
    )(order, spot, grad_mixed, normed, made, logs)


def normed_back(order, grad_made, halves):
    total, columns = grad_made.shape
    width = 2 * halves[0].shape[0] * halves[0].shape[1]
    rows = total // 2

    def kernel(order, grad_made, near, far, own, other, weight, sems):
        block_copies(order, weight, (near, far), sems, True)
        block_waits(weight, (near, far), sems, True)
        other[...] = product_transposed(grad_made[pl.ds(rows, rows), :], weight[...]).astype(bf16)
        own[...] = product_transposed(grad_made[pl.ds(0, rows), :], weight[...])

    return pl.pallas_call(
        kernel,
        in_specs=[scalars, in_vmem, anywhere, anywhere],
        out_specs=[in_vmem] * 2,
        out_shape=[
            jax.ShapeDtypeStruct((rows, width), f32),
            jax.ShapeDtypeStruct((rows, width), bf16),
        ],
        scratch_shapes=[
            pltpu.VMEM((width, columns), bf16),
            pltpu.SemaphoreType.DMA((2 * halves[0].shape[0],)),
        ],
        compiler_params=room,
        cost_estimate=no_cost,
    )(order, grad_made, *halves)


class Experts:
    def __init__(self, held, cores, groups, rows, capacity):
        self.held, self.cores, self.groups = held, cores, groups
        self.rows, self.capacity = rows, capacity

    def fetch(self, spots, shares, weight, sems, k):
        return [
            pltpu.make_async_copy(
                shares.at[spots[k, c]], weight.at[k % 2, c], sems.at[k % 2, c]
            )
            for c in range(self.cores)
        ]

    def weights_of(self, step, spots, shares, weight, sems):
        for k in range(self.held):

            @pl.when(step == k)
            def _():
                if k == 0:
                    for copy in self.fetch(spots, shares, weight, sems, 0):
                        copy.start()
                if k + 1 < self.held:
                    for copy in self.fetch(spots, shares, weight, sems, k + 1):
                        copy.start()

    def wait_weights(self, step, spots, shares, weight, sems):
        for k in range(self.held):

            @pl.when(step == k)
            def _():
                for copy in self.fetch(spots, shares, weight, sems, k):
                    copy.wait()

    def taken(self, position, k, g):
        return slot_matrix(position[k, g : g + 1, :], self.capacity)

    def dispatch(self, position, tokens, into):
        for g in range(self.groups):
            found = [self.taken(position, k, g).astype(bf16) for k in range(self.held)]
            found = jnp.concatenate(found, axis=0)
            found = product(found, tokens[pl.ds(g * self.rows, self.rows), :]).astype(bf16)
            for k in range(self.held):
                part = found[k * self.capacity : (k + 1) * self.capacity]
                into[k, pl.ds(g * self.capacity, self.capacity), :] = part

    def scales(self, position, gate, step):
        columns = []
        for g in range(self.groups):
            taken = slot_matrix(position[step, pl.ds(g, 1), :], self.capacity)
            gates = jnp.where(taken, gate[step, pl.ds(g, 1), :], 0.0)
            columns.append(jnp.sum(gates, axis=1, keepdims=True))
        return jnp.concatenate(columns, axis=0)

    def keep(self, made, step, into):
        for g in range(self.groups):
            part = made[g * self.capacity : (g + 1) * self.capacity]
            at = pl.ds(pl.multiple_of(step * self.capacity, self.capacity), self.capacity)
            into[g, at, :] = part

    def combine(self, position, made, init, slots, sems, write):
        def start(g):
            return pltpu.make_async_copy(init.at[g], slots.at[g % 2], sems.at[g % 2])

        start(0).start()
        for g in range(self.groups):
            if g + 1 < self.groups:
                start(g + 1).start()
            found = [self.taken(position, k, g).astype(bf16) for k in range(self.held)]
            found = dot_rows(jnp.concatenate(found, axis=0), made[g])
            start(g).wait()
            write(g, found + slots[g % 2])


def experts_forward(position, gate, spots, capacity, tokens, shares, init):
    (held, groups, rows), (_, _, width, hidden) = position.shape, shares.shape
    cores, slots = spots.shape[1], groups * capacity
    plan = Experts(held, cores, groups, rows, capacity)

    def kernel(spots, position, gate, tokens, shares, init, out, work, pre, weight, rows_all, made, sums, sems, sum_sems):
        step = pl.program_id(0)
        plan.weights_of(step, spots, shares, weight, sems)

        @pl.when(step == 0)
        def _():
            plan.dispatch(position, tokens, rows_all)

        plan.wait_weights(step, spots, shares, weight, sems)
        slot = lax.rem(step, 2)
        mine = rows_all[step]
        work[0] = mine
        produced = 0.0
        for c in range(cores):
            pre_gate = product(mine, weight[slot, c, 0])
            pre_up = product(mine, weight[slot, c, 1])
            pre[0, c, 0], pre[0, c, 1] = pre_gate, pre_up
            act = (pre_gate * (1.0 / (1.0 + jnp.exp(-pre_gate))) * pre_up).astype(bf16)
            produced = produced + product_transposed(act, weight[slot, c, 2])
        plan.keep((produced * plan.scales(position, gate, step)).astype(bf16), step, made)

        @pl.when(step == held - 1)
        def _():
            def write(g, total):
                out[g] = total.astype(bf16)

            plan.combine(position, made, init, sums, sum_sems, write)

    whole = pl.BlockSpec(position.shape, lambda j: (0, 0, 0))
    return pl.pallas_call(
        kernel,
        grid=(held,),
        in_specs=[
            scalars,
            whole,
            whole,
            pl.BlockSpec(tokens.shape, lambda j: (0, 0), pipeline_mode=pl.Buffered(1)),
            anywhere,
            anywhere,
        ],
        out_specs=[
            pl.BlockSpec((groups, rows, width), lambda j: (0, 0, 0)),
            pl.BlockSpec((1, slots, width), lambda j: (j, 0, 0)),
            pl.BlockSpec((1, cores, 2, slots, hidden), lambda j: (j, 0, 0, 0, 0)),
        ],
        out_shape=[
            jax.ShapeDtypeStruct((groups, rows, width), bf16),
            jax.ShapeDtypeStruct((held, slots, width), bf16),
            jax.ShapeDtypeStruct((held, cores, 2, slots, hidden), f32),
        ],
        scratch_shapes=[
            pltpu.VMEM((2, cores, 3, width, hidden), bf16),
            pltpu.VMEM((held, slots, width), bf16),
            pltpu.VMEM((groups, held * capacity, width), bf16),
            pltpu.VMEM((2, rows, width), f32),
            pltpu.SemaphoreType.DMA((2, cores)),
            pltpu.SemaphoreType.DMA((2,)),
        ],
        compiler_params=room,
        cost_estimate=no_cost,
    )(spots, position, gate, tokens, shares, init.reshape(groups, rows, width))


def experts_backward(position, gate, spots, capacity, tokens, work, pre, shares, init):
    (held, groups, rows), (_, _, width, hidden) = position.shape, shares.shape
    cores, slots = spots.shape[1], groups * capacity
    plan = Experts(held, cores, groups, rows, capacity)

    def kernel(
        spots, position, gate, tokens, work, pre, shares, init, out, grads, weight, rows_all, made, sums, fresh,
        found, sems, sum_sems, out_sems,
    ):
        step = pl.program_id(0)
        plan.weights_of(step, spots, shares, weight, sems)

        @pl.when(step == 0)
        def _():
            plan.dispatch(position, tokens, rows_all)

        plan.wait_weights(step, spots, shares, weight, sems)
        slot = lax.rem(step, 2)
        scale = plan.scales(position, gate, step)
        mine, produced, chosen, acts, pres = rows_all[step], 0.0, 0.0, [], []
        for c in range(cores):
            back = product(mine, weight[slot, c, 2])
            pre_gate, pre_up = pre[0, c, 0], pre[0, c, 1]
            logistic = 1.0 / (1.0 + jnp.exp(-pre_gate))
            activated = pre_gate * logistic * pre_up
            chosen = chosen + jnp.sum(back * activated, axis=1, keepdims=True)
            acts.append((activated * scale).astype(bf16))
            back = back * scale
            grad_gate = back * pre_up * logistic * (1.0 + pre_gate * (1.0 - logistic))
            pres.append((grad_gate.astype(bf16), (back * pre_gate * logistic).astype(bf16)))
            for s in range(2):
                produced = produced + product_transposed(pres[c][s], weight[slot, c, s])
        plan.keep(produced.astype(bf16), step, made)
        for g in range(groups):
            taken = slot_matrix(position[step, pl.ds(g, 1), :], capacity)
            part = chosen[g * capacity : (g + 1) * capacity]
            found[step, pl.ds(g, 1), :] = jnp.sum(jnp.where(taken, part, 0.0), axis=0, keepdims=True)

        def store(k):
            return [
                pltpu.make_async_copy(fresh.at[c], grads.at[spots[k, c]], out_sems.at[c])
                for c in range(cores)
            ]

        for k in range(1, held):

            @pl.when(step == k)
            def _():
                for copy in store(k - 1):
                    copy.wait()

        for c in range(cores):
            for s in range(2):
                fresh[c, s] = dot_rows(work[0], pres[c][s]).astype(bf16)
            fresh[c, 2] = dot_rows(mine, acts[c]).astype(bf16)
        for k in range(held):

            @pl.when(step == k)
            def _():
                for copy in store(k):
                    copy.start()

        @pl.when(step == held - 1)
        def _():
            def write(g, total):
                out[g, pl.ds(0, rows), :] = total.astype(bf16)
                tail = jnp.concatenate([found[k, g : g + 1, :] for k in range(held)], axis=0)
                high = tail.astype(bf16).astype(f32)
                tail = [high, tail - high, jnp.zeros((TAIL - 2 * held, rows), f32)]
                out[g, pl.ds(rows, TAIL), pl.ds(0, rows)] = jnp.concatenate(tail, axis=0).astype(bf16)

            plan.combine(position, made, init, sums, sum_sems, write)
            for copy in store(held - 1):
                copy.wait()

    whole = pl.BlockSpec(position.shape, lambda j: (0, 0, 0))
    return pl.pallas_call(
        kernel,
        grid=(held,),
        in_specs=[
            scalars,
            whole,
            whole,
            pl.BlockSpec(tokens.shape, lambda j: (0, 0), pipeline_mode=pl.Buffered(1)),
            pl.BlockSpec((1, slots, width), lambda j: (j, 0, 0)),
            pl.BlockSpec((1, cores, 2, slots, hidden), lambda j: (j, 0, 0, 0, 0)),
            anywhere,
            anywhere,
        ],
        out_specs=[pl.BlockSpec((groups, rows + TAIL, width), lambda j: (0, 0, 0)), anywhere],
        out_shape=[
            jax.ShapeDtypeStruct((groups, rows + TAIL, width), bf16),
            jax.ShapeDtypeStruct(shares.shape, bf16),
        ],
        scratch_shapes=[
            pltpu.VMEM((2, cores, 3, width, hidden), bf16),
            pltpu.VMEM((held, slots, width), bf16),
            pltpu.VMEM((groups, held * capacity, width), bf16),
            pltpu.VMEM((2, rows, width), f32),
            pltpu.VMEM((cores, 3, width, hidden), bf16),
            pltpu.VMEM(position.shape, f32),
            pltpu.SemaphoreType.DMA((2, cores)),
            pltpu.SemaphoreType.DMA((2,)),
            pltpu.SemaphoreType.DMA((cores,)),
        ],
        compiler_params=room,
        cost_estimate=no_cost,
    )(spots, position, gate, tokens, work, pre, shares, init.reshape(groups, rows, width))


def spread_shared(lay, shared_in, shared_out, member):
    rows, hidden = shared_out.shape
    part = hidden // len(lay.g_masks)
    stacked = jnp.concatenate([shared_in, shared_out[None]], axis=0)
    stacked = stacked.reshape(3 * rows, hidden)
    member_rows = member.reshape(-1, part)

    def piece(mask):
        chunk = lax.dynamic_slice_in_dim(stacked, lay.chunk(mask) * part, part, 1)
        return jnp.concatenate([chunk, member_rows], axis=0)

    pieces = [piece(0)] + [lay.shift(piece(m), m) for m in lay.g_masks[1:]]
    chunks = jnp.stack([p[: 3 * rows].reshape(3, rows, part) for p in pieces])
    return chunks, jnp.stack([p[3 * rows :].reshape(member.shape) for p in pieces])


def gather_shared(lay, blocks):
    _, _, matrices, rows, part = (len(blocks),) + blocks[0].shape
    everyone = jnp.stack(blocks, axis=1)
    natural = everyone.reshape((lay.dp, matrices, rows, part))[lay.rows_order()]
    return natural.transpose(1, 0, 2, 3).reshape(matrices, lay.dp * rows, part)


def scatter_shared(lay, grads, after):
    part = grads.shape[2] // lay.tp
    rows = grads.shape[1] // lay.dp
    own = lay.scatter_core([grads[:, :, k * part : (k + 1) * part] for k in range(lay.tp)])
    natural = own.astype(bf16).reshape(3, lay.dp, rows, part).transpose(1, 0, 2, 3)
    blocks = natural[lay.rows_apart()].reshape(len(lay.g_masks), len(lay.w_masks), 3, rows, part)
    summed = lay.scatter_w([blocks[:, k] for k in range(len(lay.w_masks))], after[0])
    summed = behind(summed, after[2])
    out = jnp.zeros((3, rows, part * len(lay.g_masks)), f32)
    for k, mask in enumerate(lay.g_masks):
        got = summed[k] if k == 0 else lay.shift(summed[k].astype(bf16), mask).astype(f32)
        out = lax.dynamic_update_slice_in_dim(out, got, lay.chunk(mask) * part, 2)
    return out


def scatter_parts(lay, parts):
    return [lay.shift(part, mask) if mask else part for part, mask in zip(parts, lay.g_masks)]


def on_device(
    block_input,
    teacher,
    lengths,
    routes,
    gain_attn,
    w_query,
    key_value_weight,
    w_out,
    gain_moe,
    w_router,
    w_shared_in,
    w_shared_out,
    w_expert_in,
    w_expert_out,
):
    lay = Layout()
    own_rows, width = block_input.shape
    tp, dp = lay.tp, lay.dp
    sequence_length = own_rows * tp
    experts = w_expert_in.shape[0] * dp
    capacity = max(2, own_rows * TOPK * 4 // (3 * experts))
    n_g, n_w = len(lay.g_masks), len(lay.w_masks)
    length = lengths[lay.place]
    slices = jnp.array(range(tp), jnp.int32) ^ lay.core
    positions = (slices[:, None] * own_rows + jnp.arange(own_rows)[None, :]).reshape(-1)
    own_valid = (positions[:own_rows] < length).astype(f32)[:, None]
    head_count = w_query.shape[1] // HEAD_SIZE
    kv_count = key_value_weight.shape[2] // HEAD_SIZE
    head_group = head_count // kv_count
    q_dim, kv_dim = head_count * HEAD_SIZE, kv_count * HEAD_SIZE
    in_kernel = n_g * own_rows <= 1024
    forward = experts_forward if in_kernel else experts_forward_plain
    backward = experts_backward if in_kernel else experts_backward_plain

    own_routes = lax.dynamic_slice_in_dim(routes, lay.core * own_rows, own_rows, 0)
    expert_ids = jnp.arange(experts, dtype=jnp.int32)
    member = jnp.any(own_routes.T[None, :, :] == expert_ids[:, None, None], axis=1)
    held_ids = lay.place ^ jnp.array(lay.w_masks, jnp.int32)
    held_hot = (held_ids[:, None] == expert_ids).astype(f32)
    shared_parts, group_member = spread_shared(
        lay, w_shared_in, w_shared_out, member.astype(bf16)
    )
    held_member = contract("je,get->jgt", held_hot.astype(bf16), group_member)
    before = jnp.triu(jnp.ones((own_rows, own_rows), bf16), 1)
    position = contract("jgu,ut->jgt", held_member.astype(bf16), before)
    position = jnp.where(held_member > 0, position, -1.0)

    near, far = (1 << bit for bit in lay.w_bits)
    input_slices = lay.gather_core(block_input)
    qkv = Tree(lay, jnp.concatenate([w_query, key_value_weight[0], key_value_weight[1]], axis=1))
    router_pad = jnp.zeros((w_router.shape[0], -experts % 128), bf16)
    out = Tree(lay, jnp.concatenate([w_out, w_router, router_pad], axis=1))
    expert_shares = lax.all_gather(
        jnp.concatenate([w_expert_in[0], w_expert_out], axis=0),
        ("dp", "tensor"),
        axis_index_groups=lay.w_groups(),
    )
    steps = len(lay.steps)
    qkv.step()
    out.step(qkv.marks[0])
    qkv.step(shared_parts, input_slices, group_member)
    shared_far = lay.shift(behind(shared_parts, out.marks[0]), far)
    out.step(qkv.marks[1])
    for k in range(2, steps):
        gates = [out.marks[min(k - 2, 1)]] + ([shared_far] if k == steps - 1 else [])
        qkv.step(*gates)
    for k in range(2, steps):
        out.step(qkv.marks[-1])
    shared_near = lay.shift(behind(jnp.stack([shared_parts, shared_far]), qkv.marks[-1]), near)

    spot = jnp.stack([lay.core, length]).astype(jnp.int32)
    in_order = lay.gather_order()
    residual = block_input.astype(f32)
    _, scale_attn = normalize_rows(residual, gain_attn)

    def by_core(rows):
        return [rows[k * own_rows : (k + 1) * own_rows] for k in range(tp)]

    if in_kernel:
        normed_all, projected, mixed_heads, logs = attend(
            in_order, spot, *input_slices, gain_attn, qkv.halves, head_count, kv_count
        )
        *attn_parts, out_router = project_out(
            behind(in_order, shared_near), mixed_heads, out.halves
        )
    else:
        qkv_full, out_router = lay.in_order(qkv.halves), lay.in_order(out.halves)
        normed_all, _ = normalize_rows(
            jnp.concatenate(input_slices, axis=0).astype(f32), gain_attn
        )
        projected = product(normed_all, qkv_full).astype(bf16)
        queries = projected[:, :q_dim].reshape(sequence_length, kv_count, head_group, HEAD_SIZE)
        key_row_table = projected[:, q_dim : q_dim + kv_dim].reshape(
            sequence_length, kv_count, HEAD_SIZE
        )
        value_row_table = projected[:, q_dim + kv_dim :].reshape(
            sequence_length, kv_count, HEAD_SIZE
        )
        allowed = (positions[None, :] <= positions[:, None]) & (positions[None, :] < length)
        scores = contract("qvgd,kvd->vgqk", queries, key_row_table) * HEAD_SIZE ** (-0.5)
        scores = jnp.where(allowed, scores, masked_score)
        row_max = jnp.max(scores, axis=-1, keepdims=True)
        exponent_terms = jnp.exp(scores - row_max)
        row_sum = jnp.sum(exponent_terms, axis=-1, keepdims=True)
        probs_full = exponent_terms / row_sum
        probs_low = probs_full.astype(bf16)
        mixed_heads = (
            contract("vgqk,kvd->qvgd", probs_low, value_row_table)
            .astype(bf16)
            .reshape(sequence_length, q_dim)
        )
        attn_parts = by_core(product_transposed(mixed_heads, out_router[:, :q_dim]))
    router_full = out_router[:, q_dim : q_dim + experts]
    hidden = residual + lay.scatter_core(attn_parts)
    moe_own, scale_moe = normalize_rows(hidden, gain_moe)

    arrived = lay.gather_g(moe_own)
    shared_own = gather_shared(lay, [shared_parts, shared_near[0], shared_far, shared_near[1]])
    shared_full = jnp.concatenate(lay.gather_core(shared_own), axis=2)
    shared_in_full, shared_out_full = shared_full[:2], shared_full[2]

    group_rows = jnp.concatenate(arrived, axis=0)
    logits = lax.dot_general(
        router_full, group_rows, (((0,), (1,)), ((), ())), preferred_element_type=f32
    )
    shown = jnp.where(
        group_member.transpose(1, 0, 2).reshape(experts, -1) > 0, logits, masked_score
    )
    gate_terms = jnp.exp(shown - jnp.max(shown, axis=0, keepdims=True))
    gates = gate_terms / jnp.sum(gate_terms, axis=0, keepdims=True)
    own_gates = gates[:, :own_rows]
    held_gates = jnp.sum(held_hot[:, :, None] * gates[None], axis=1).reshape(n_w, n_g, own_rows)
    shared_pre = contract("td,cdf->ctf", group_rows, shared_in_full)
    shared_act = (jax.nn.silu(shared_pre[0]) * shared_pre[1]).astype(bf16)
    total = product_transposed(shared_act, shared_out_full)
    spots = lay.w_spots()
    total, work, pre = forward(
        position, held_gates, spots, capacity, group_rows, expert_shares, total
    )

    def scatter_g(parts):
        return sum(part.astype(f32) for part in scatter_parts(lay, parts))

    out_rows = (hidden + scatter_g([total[k] for k in range(n_g)])) * own_valid
    residual_error = (out_rows - teacher.astype(f32)) * own_valid
    loss_part = 0.5 * jnp.sum(residual_error * residual_error)

    group_grad = jnp.concatenate(lay.gather_g(residual_error.astype(bf16)), axis=0)
    grad_shared_act = product(group_grad, shared_out_full)
    grad_shared_out = product_left(group_grad, shared_act)
    grad_shared_pre = jnp.stack(swish_back(shared_pre[0], shared_pre[1], grad_shared_act))
    grad_shared_in = contract("td,ctf->cdf", group_rows, grad_shared_pre)
    total = contract("ctf,cdf->td", grad_shared_pre, shared_in_full)
    total, grad_shares = backward(
        position, held_gates, spots, capacity, group_grad, work, pre, expert_shares, total
    )
    grad_expert = lax.psum_scatter(
        grad_shares, ("dp", "tensor"), axis_index_groups=lay.w_groups()
    ).astype(f32)
    received = scatter_parts(lay, [total[k] for k in range(n_g)])
    returned = received[0][:own_rows].astype(f32)
    for part in received[1:]:
        returned = returned + part[:own_rows].astype(f32)
    gate_rows = [part[own_rows:, :own_rows].astype(f32) for part in received]
    gate_rows = [rows[:n_w] + rows[n_w : 2 * n_w] for rows in gate_rows]
    ids = lay.place ^ jnp.array([g ^ w for g in lay.g_masks for w in lay.w_masks], jnp.int32)
    placed = (expert_ids[:, None] == ids).astype(f32)[:, :, None]
    grad_gates = jnp.sum(placed * jnp.concatenate(gate_rows, axis=0)[None], axis=1)
    grad_logits = (
        own_gates * (grad_gates - jnp.sum(own_gates * grad_gates, axis=0, keepdims=True))
    ).astype(bf16)
    grad_router_part = lax.dot_general(
        moe_own, grad_logits, (((0,), (1,)), ((), ())), preferred_element_type=f32
    )
    grad_normed_own = returned + lax.dot_general(
        grad_logits, router_full, (((0,), (1,)), ((), ())), preferred_element_type=f32
    )

    grad_from_moe, grad_gain_moe_part = normalize_back(hidden, scale_moe, gain_moe, grad_normed_own)
    grad_hidden = residual_error + grad_from_moe
    grad_slices = lay.gather_core(grad_hidden.astype(bf16))
    grad_router_part = jnp.pad(
        lay.scatter_core([grad_router_part] * tp).astype(bf16), ((0, 0), (0, -experts % 128))
    )
    if in_kernel:
        grad_mixed, *out_back_halves = project_out_back(
            lay.scatter_order(), *grad_slices, out_router, mixed_heads, grad_router_part
        )
        grad_projected, *qkv_back_halves = attend_back(
            lay.scatter_order(), spot, grad_mixed, normed_all, projected, logs, head_count, kv_count
        )
        normed_parts = normed_back(in_order, grad_projected, qkv.halves)
    else:
        grad_attn = jnp.concatenate(grad_slices, axis=0)
        grad_mixed = (
            product(grad_attn, out_router[:, :q_dim])
            .astype(bf16)
            .reshape(sequence_length, kv_count, head_group, HEAD_SIZE)
        )
        grad_values = contract("vgqk,qvgd->kvd", probs_low, grad_mixed)
        grad_probs = contract("qvgd,kvd->vgqk", grad_mixed, value_row_table)
        delta_sum = jnp.sum(probs_full * grad_probs, axis=-1, keepdims=True)
        grad_scores = (probs_full * (grad_probs - delta_sum)).astype(bf16)
        grad_queries = contract("vgqk,kvd->qvgd", grad_scores, key_row_table) * HEAD_SIZE ** (-0.5)
        grad_keys = contract("vgqk,qvgd->kvd", grad_scores, queries) * HEAD_SIZE ** (-0.5)
        grad_projected = jnp.concatenate(
            [
                grad_queries.astype(bf16).reshape(sequence_length, q_dim),
                grad_keys.astype(bf16).reshape(sequence_length, kv_dim),
                grad_values.astype(bf16).reshape(sequence_length, kv_dim),
            ],
            axis=1,
        )
        out_back_halves = lay.in_halves(
            jnp.concatenate([product_left(grad_attn, mixed_heads).astype(bf16), grad_router_part], axis=1)
        )
        qkv_back_halves = lay.in_halves(product_left(normed_all, grad_projected))
        normed_parts = by_core(product_transposed(grad_projected, qkv_full))
    out_back = Sum(lay, out_back_halves)
    keep, send = qkv_back_halves
    send = behind(send, out_back.step(grad_projected))
    qkv_back = Sum(lay, (keep, send))
    qkv_back.step()
    for k in range(1, steps):
        out_back.step(qkv_back.marks[k - 1] if k > 1 else grad_projected)
        qkv_back.step()
    grad_qkv, grad_out_router = qkv_back.total[0], out_back.total[0]
    qkv_back = qkv_back.marks
    grad_normed_attn = lay.scatter_core(normed_parts)
    grad_from_attn, grad_gain_attn_part = normalize_back(
        residual, scale_attn, gain_attn, grad_normed_attn
    )
    input_grad = grad_hidden + grad_from_attn
    grad_w_kv = jnp.stack(
        [grad_qkv[:, q_dim : q_dim + kv_dim], grad_qkv[:, q_dim + kv_dim :]], axis=0
    )
    small = jnp.stack(
        [grad_gain_attn_part, grad_gain_moe_part, jnp.full((width,), loss_part, f32)], axis=0
    )
    small = lay.sum_all(small, qkv_back)
    loss = small[2, 0] / (jnp.sum(lengths).astype(f32) * width)
    grad_shared = scatter_shared(
        lay, jnp.concatenate([grad_shared_in, grad_shared_out[None]]), qkv_back
    )
    return (
        out_rows.astype(bf16),
        loss,
        input_grad,
        small[0],
        grad_qkv[:, :q_dim],
        grad_w_kv,
        grad_out_router[:, :q_dim],
        small[1],
        grad_out_router[:, q_dim : q_dim + experts],
        grad_shared[:2],
        grad_shared[2],
        grad_expert[None, :2],
        grad_expert[2:],
    )


def solution(mesh):
    rows, weights = P(("dp", "tensor"), None), P("dp", "tensor")
    stacked = P(None, "dp", "tensor")
    expert_in, expert_out = P("dp", None, None, "tensor"), P("dp", None, "tensor")
    return jax.shard_map(
        on_device,
        mesh=mesh,
        in_specs=(
            rows,
            rows,
            P(),
            P("dp", None),
            P(),
            weights,
            stacked,
            weights,
            P(),
            P("dp", None),
            stacked,
            weights,
            expert_in,
            expert_out,
        ),
        out_specs=(
            rows,
            P(),
            rows,
            P(),
            weights,
            stacked,
            weights,
            P(),
            P("dp", None),
            stacked,
            weights,
            expert_in,
            expert_out,
        ),
        check_vma=False,
    )
```

```python
import jax
import jax.numpy as jnp
from jax import lax
from jax.experimental import pallas as pl
from jax.experimental.pallas import tpu as pltpu
from jax.sharding import PartitionSpec as P

HEAD_SIZE = 128
TOPK = 6

norm_eps = 1e-05
masked_score = -1e30
TAIL = 16
bf16 = jnp.bfloat16
f32 = jnp.float32


def product(left_side, right_side):
    return jnp.dot(left_side, right_side, preferred_element_type=f32)


def product_transposed(left_side, right_side):
    return lax.dot_general(
        left_side, right_side, (((1,), (1,)), ((), ())), preferred_element_type=f32
    )


def product_left(left_side, right_side):
    return lax.dot_general(
        left_side, right_side, (((0,), (0,)), ((), ())), preferred_element_type=f32
    )


def contract(spec, *operands):
    return jnp.einsum(spec, *operands, preferred_element_type=f32)


def normalize_rows(values, gain):
    row_scale = lax.rsqrt(jnp.mean(values * values, axis=-1, keepdims=True) + norm_eps)
    return ((values * row_scale * gain).astype(bf16), row_scale)


def normalize_back(values, row_scale, gain, grad_normed):
    scaled = grad_normed * gain
    inner_mean = jnp.mean(scaled * values, axis=-1, keepdims=True)
    grad_values = row_scale * (scaled - values * row_scale * row_scale * inner_mean)
    grad_gain = jnp.sum(grad_normed * values * row_scale, axis=0)
    return (grad_values, grad_gain)


def swish_back(pre_gate, pre_up, grad_act):
    logistic = jax.nn.sigmoid(pre_gate)
    grad_gate = grad_act * pre_up * logistic * (1.0 + pre_gate * (1.0 - logistic))
    grad_up = grad_act * pre_gate * logistic
    return grad_gate.astype(bf16), grad_up.astype(bf16)


def subset_masks(bits):
    masks = [0]
    for bit in bits:
        masks = masks + [mask | (1 << bit) for mask in masks]
    return masks


def behind(values, *others):
    return lax.optimization_barrier((values,) + others)[0]


class Tree:
    def __init__(self, lay, shard):
        self.lay, self.halves, self.marks = lay, (shard[None],), []

    def step(self, *others):
        held = jnp.concatenate(self.halves, axis=0)
        if others:
            held = behind(held, *others)
        self.marks.append(self.lay.shift(held, 1 << self.lay.tree_bits[len(self.marks)]))
        self.halves = (held, self.marks[-1])
        return self.marks[-1]


class Sum:
    def __init__(self, lay, halves):
        self.lay, (self.keep, self.send), self.marks = lay, halves, []

    def step(self, *others):
        got = self.lay.shift(self.send, 1 << self.lay.tree_bits[-1 - len(self.marks)])
        if others:
            got = behind(got, *others)
        self.marks.append(got)
        self.total = self.keep.astype(f32) + got.astype(f32)
        half = self.total.shape[0] // 2
        self.keep, self.send = self.total[:half], self.total[half:].astype(bf16)
        return got


class Layout:
    def __init__(self):
        self.dp = lax.axis_size("dp")
        self.tp = lax.axis_size("tensor")
        self.place = lax.axis_index("dp")
        self.core = lax.axis_index("tensor")
        bits = self.dp.bit_length() - 1
        self.w_bits = [bit for bit in (1, 3) if bit < bits]
        self.g_bits = [bit for bit in range(bits) if bit not in self.w_bits]
        self.w_masks = subset_masks(self.w_bits)
        self.g_masks = subset_masks(self.g_bits)
        self.tree_bits = list(range(bits - 1, -1, -1))

    def shift(self, values, mask):
        return lax.ppermute(values, "dp", [(i, i ^ mask) for i in range(self.dp)])

    def w_groups(self):
        groups = []
        for i in range(self.dp):
            if all(i & mask == 0 for mask in self.w_masks):
                places = sorted(i ^ mask for mask in self.w_masks)
                groups.append([place * self.tp + c for place in places for c in range(self.tp)])
        return groups

    def w_spots(self):
        bits = [(self.place >> bit) & 1 for bit in self.w_bits]
        rows = []
        for k in range(len(self.w_masks)):
            spot = sum((bit ^ ((k >> n) & 1)) << n for n, bit in enumerate(bits))
            rows.append(jnp.stack([spot * self.tp + (self.core ^ c) for c in range(self.tp)]))
        return jnp.stack(rows).astype(jnp.int32)

    def shift_core(self, values, mask):
        return lax.ppermute(values, "tensor", [(i, i ^ mask) for i in range(self.tp)])

    def tree_order(self):
        apart = self.place ^ jnp.arange(self.dp)
        return sum(((apart >> bit) & 1) << k for k, bit in enumerate(self.tree_bits))

    def in_order(self, halves):
        whole = jnp.concatenate(halves, axis=0)[self.tree_order()]
        return whole.reshape((-1,) + whole.shape[2:])

    def in_halves(self, whole):
        blocks = whole.astype(bf16).reshape((self.dp, -1) + whole.shape[1:])
        rel = jnp.arange(self.dp)
        apart = sum(((rel >> k) & 1) << bit for k, bit in enumerate(self.tree_bits))
        at = self.place ^ apart
        return blocks[at[: self.dp // 2]], blocks[at[self.dp // 2 :]]

    def gather_g(self, values):
        return [values] + [self.shift(values, mask) for mask in self.g_masks[1:]]

    def scatter_w(self, blocks, after):
        near, far = (1 << bit for bit in self.w_bits)
        both = jnp.stack([blocks[3], blocks[1]]).astype(bf16)
        far_one, own = behind(self.shift(both, near), after)
        far_one = self.shift((blocks[2].astype(f32) + far_one.astype(f32)).astype(bf16), far)
        return blocks[0].astype(f32) + own.astype(f32) + far_one.astype(f32)

    def gather_core(self, values):
        return [values] + [self.shift_core(values, k) for k in range(1, self.tp)]

    def scatter_core(self, blocks):
        total = blocks[0].astype(f32)
        for k in range(1, self.tp):
            total = total + self.shift_core(blocks[k].astype(bf16), k).astype(f32)
        return total

    def sum_all(self, values, marks):
        for bit, mark in enumerate(marks):
            values = behind(values, mark)
            values = values + self.shift(values, 1 << bit)
        for bit in range(self.tp.bit_length() - 1):
            values = values + self.shift_core(values, 1 << bit)
        return values

    def chunk(self, mask):
        place = self.place ^ mask
        return sum(((place >> bit) & 1) << k for k, bit in enumerate(self.g_bits))

    def rows_order(self):
        apart = self.place ^ jnp.arange(self.dp)
        g = sum(((apart >> bit) & 1) << k for k, bit in enumerate(self.g_bits))
        w = sum(((apart >> bit) & 1) << k for k, bit in enumerate(self.w_bits))
        return g * len(self.w_masks) + w

    def rows_apart(self):
        masks = jnp.array([g | w for g in self.g_masks for w in self.w_masks], jnp.int32)
        return self.place ^ masks


def slots_of(position, capacity):
    slots = jnp.arange(capacity, dtype=f32)[:, None]
    return (position[:, :, None, :] == slots).astype(bf16)


def experts_forward_plain(position, gate, spots, capacity, tokens, shares, init):
    (held, groups, rows), width = position.shape, tokens.shape[1]
    taken = slots_of(position, capacity)
    work = contract("jgct,gtd->jgcd", taken, tokens.reshape(groups, rows, width)).astype(bf16)
    work = work.reshape(held, groups * capacity, width)
    scale = jnp.sum(taken.astype(f32) * gate[:, :, None, :], axis=-1).reshape(held, -1, 1)
    pre, made = [], 0.0
    for c in range(spots.shape[1]):
        weight = shares[spots[:, c]]
        pre.append(contract("jrd,jsdf->jsrf", work, weight[:, :2]))
        act = (jax.nn.silu(pre[-1][:, 0]) * pre[-1][:, 1]).astype(bf16)
        made = made + contract("jrf,jdf->jrd", act, weight[:, 2])
    made = (made * scale).astype(bf16).reshape(held, groups, capacity, width)
    total = init.reshape(groups, rows, width) + contract("jgct,jgcd->gtd", taken, made)
    return total.astype(bf16), work, jnp.stack(pre, axis=1)


def experts_backward_plain(position, gate, spots, capacity, tokens, work, pre, shares, init):
    (held, groups, rows), width = position.shape, tokens.shape[1]
    taken = slots_of(position, capacity)
    grad_rows = contract("jgct,gtd->jgcd", taken, tokens.reshape(groups, rows, width)).astype(bf16)
    grad_rows = grad_rows.reshape(held, groups * capacity, width)
    scale = jnp.sum(taken.astype(f32) * gate[:, :, None, :], axis=-1).reshape(held, -1, 1)
    chosen, made, grads = 0.0, 0.0, jnp.zeros(shares.shape, bf16)
    for c in range(spots.shape[1]):
        weight = shares[spots[:, c]]
        back = contract("jrd,jdf->jrf", grad_rows, weight[:, 2])
        activated = jax.nn.silu(pre[:, c, 0]) * pre[:, c, 1]
        chosen = chosen + jnp.sum(back * activated, axis=-1)
        grad_pre = jnp.stack(swish_back(pre[:, c, 0], pre[:, c, 1], back * scale), axis=1)
        made = made + contract("jsrf,jsdf->jrd", grad_pre, weight[:, :2])
        grad_in = contract("jrd,jsrf->jsdf", work, grad_pre).astype(bf16)
        grad_out = contract("jrd,jrf->jdf", grad_rows, (activated * scale).astype(bf16)).astype(bf16)
        grads = grads.at[spots[:, c]].set(jnp.concatenate([grad_in, grad_out[:, None]], axis=1))
    made = made.astype(bf16).reshape(held, groups, capacity, width)
    total = init.reshape(groups, rows, width) + contract("jgct,jgcd->gtd", taken, made)
    chosen = jnp.sum(taken.astype(f32) * chosen.reshape(held, groups, capacity, 1), axis=2)
    tail = chosen.transpose(1, 0, 2)
    high = tail.astype(bf16).astype(f32)
    tail = jnp.concatenate([high, tail - high], axis=1)
    tail = jnp.pad(tail, ((0, 0), (0, TAIL - tail.shape[1]), (0, width - rows)))
    return jnp.concatenate([total, tail], axis=1).astype(bf16), grads


def dot_rows(left, right):
    return lax.dot_general(left, right, (((0,), (0,)), ((), ())), preferred_element_type=f32)


def slot_matrix(position, capacity):
    slots = lax.broadcasted_iota(jnp.int32, (capacity, position.shape[1]), 0).astype(f32)
    return slots == position


def block_copies(order, whole, halves, sems, inward):
    blocks, rows = halves[0].shape[0], halves[0].shape[1]
    for i in range(2 * blocks):
        part = whole.at[pl.ds(i * rows, rows)]
        for k, half in enumerate(halves):

            @pl.when((order[i] >= k * blocks) & (order[i] < (k + 1) * blocks))
            def _():
                block = half.at[order[i] - k * blocks]
                source, target = (block, part) if inward else (part, block)
                pltpu.make_async_copy(source, target, sems.at[i]).start()


def block_waits(whole, halves, sems, inward):
    blocks, rows = halves[0].shape[0], halves[0].shape[1]
    for i in range(2 * blocks):
        part = whole.at[pl.ds(i * rows, rows)]
        source, target = (halves[0].at[0], part) if inward else (part, halves[0].at[0])
        pltpu.make_async_copy(source, target, sems.at[i]).wait()


def score_mask(core, length, rows):
    row = lax.broadcasted_iota(jnp.int32, (rows, rows), 0)
    col = lax.broadcasted_iota(jnp.int32, (rows, rows), 1)
    first = core * (rows // 2)
    row = jnp.where(row < rows // 2, row + first, row - first)
    col = jnp.where(col < rows // 2, col + first, col - first)
    return (col <= row) & (col < length)


anywhere = pl.BlockSpec(memory_space=pl.ANY)
scalars = pl.BlockSpec(memory_space=pltpu.SMEM)
in_vmem = pl.BlockSpec(memory_space=pltpu.VMEM)
no_cost = pl.CostEstimate(flops=0, transcendentals=0, bytes_accessed=0)
room = pltpu.CompilerParams(vmem_limit_bytes=56 * 1024 * 1024)


def attend(order, spot, own, other, gain, halves, head_count, kv_count):
    rows, width = own.shape
    total, columns = 2 * rows, halves[0].shape[2]
    group = head_count // kv_count

    def kernel(order, spot, own, other, gain, near, far, normed, made, mixed, logs, weight, sems):
        block_copies(order, weight, (near, far), sems, True)
        for k, part in enumerate((own, other)):
            values = part[...].astype(f32)
            scale = lax.rsqrt(jnp.mean(values * values, axis=1, keepdims=True) + norm_eps)
            normed[pl.ds(k * rows, rows), :] = (values * scale * gain[...]).astype(bf16)
        block_waits(weight, (near, far), sems, True)
        made[...] = product(normed[...], weight[...]).astype(bf16)
        allowed = score_mask(spot[0], spot[1], total)
        for h in range(head_count):
            key = pl.ds((head_count + h // group) * HEAD_SIZE, HEAD_SIZE)
            value = pl.ds((head_count + kv_count + h // group) * HEAD_SIZE, HEAD_SIZE)
            at = pl.ds(h * HEAD_SIZE, HEAD_SIZE)
            scores = product_transposed(made[:, at], made[:, key]) * HEAD_SIZE ** (-0.5)
            scores = jnp.where(allowed, scores, masked_score)
            most = jnp.max(scores, axis=1, keepdims=True)
            terms = jnp.exp(scores - most)
            together = jnp.sum(terms, axis=1, keepdims=True)
            probs = (terms * (1.0 / together)).astype(bf16)
            mixed[:, at] = product(probs, made[:, value]).astype(bf16)
            logs[h] = most + jnp.log(together)

    return pl.pallas_call(
        kernel,
        in_specs=[scalars, scalars, in_vmem, in_vmem, in_vmem, anywhere, anywhere],
        out_specs=[in_vmem] * 4,
        out_shape=[
            jax.ShapeDtypeStruct((total, width), bf16),
            jax.ShapeDtypeStruct((total, columns), bf16),
            jax.ShapeDtypeStruct((total, head_count * HEAD_SIZE), bf16),
            jax.ShapeDtypeStruct((head_count, total, 1), f32),
        ],
        scratch_shapes=[
            pltpu.VMEM((width, columns), bf16),
            pltpu.SemaphoreType.DMA((2 * halves[0].shape[0],)),
        ],
        compiler_params=room,
        cost_estimate=no_cost,
    )(order, spot, own, other, gain[None], *halves)


def project_out(order, mixed, halves):
    total, columns = mixed.shape
    width = 2 * halves[0].shape[0] * halves[0].shape[1]
    rows = total // 2

    def kernel(order, mixed, near, far, own, other, weight, sems):
        block_copies(order, weight, (near, far), sems, True)
        block_waits(weight, (near, far), sems, True)
        other[...] = product_transposed(mixed[pl.ds(rows, rows), :], weight[:, :columns]).astype(bf16)
        own[...] = product_transposed(mixed[pl.ds(0, rows), :], weight[:, :columns])

    return pl.pallas_call(
        kernel,
        in_specs=[scalars, in_vmem, anywhere, anywhere],
        out_specs=[in_vmem] * 3,
        out_shape=[
            jax.ShapeDtypeStruct((rows, width), f32),
            jax.ShapeDtypeStruct((rows, width), bf16),
            jax.ShapeDtypeStruct((width, halves[0].shape[2]), bf16),
        ],
        scratch_shapes=[pltpu.SemaphoreType.DMA((2 * halves[0].shape[0],))],
        compiler_params=room,
        cost_estimate=no_cost,
    )(order, mixed, *halves)


def half_shapes(places, width, columns):
    block = jax.ShapeDtypeStruct((places // 2, width // places, columns), bf16)
    return [block, block]


def project_out_back(order, own, other, weight, mixed, router):
    total, columns = mixed.shape
    rows, width = own.shape
    places = order.shape[0]

    def kernel(order, own, other, weight, mixed, router, grad_mixed, near, far, grads, both, sems):
        both[pl.ds(0, rows), :] = own[...]
        both[pl.ds(rows, rows), :] = other[...]
        grads[:, :columns] = dot_rows(both[...], mixed[...]).astype(bf16)
        grads[:, columns:] = router[...]
        block_copies(order, grads, (near, far), sems, False)
        grad_mixed[...] = product(both[...], weight[:, :columns]).astype(bf16)
        block_waits(grads, (near, far), sems, False)

    return pl.pallas_call(
        kernel,
        in_specs=[scalars] + [in_vmem] * 5,
        out_specs=[in_vmem, anywhere, anywhere],
        out_shape=[jax.ShapeDtypeStruct((total, columns), bf16)]
        + half_shapes(places, width, weight.shape[1]),
        scratch_shapes=[
            pltpu.VMEM(weight.shape, bf16),
            pltpu.VMEM((total, width), bf16),
            pltpu.SemaphoreType.DMA((places,)),
        ],
        compiler_params=room,
        cost_estimate=no_cost,
    )(order, own, other, weight, mixed, router)


def attend_back(order, spot, grad_mixed, normed, made, logs, head_count, kv_count):
    total, width = normed.shape
    columns, group = made.shape[1], head_count // kv_count
    places = order.shape[0]

    def kernel(order, spot, grad_mixed, normed, made, logs, grad_made, near, far, grads, sems):
        allowed = score_mask(spot[0], spot[1], total)
        for v in range(kv_count):
            key = pl.ds((head_count + v) * HEAD_SIZE, HEAD_SIZE)
            value = pl.ds((head_count + kv_count + v) * HEAD_SIZE, HEAD_SIZE)
            grad_key, grad_value = 0.0, 0.0
            for h in range(v * group, (v + 1) * group):
                at = pl.ds(h * HEAD_SIZE, HEAD_SIZE)
                scores = product_transposed(made[:, at], made[:, key]) * HEAD_SIZE ** (-0.5)
                probs = jnp.where(allowed, jnp.exp(scores - logs[h]), 0.0)
                grad_value = grad_value + dot_rows(probs.astype(bf16), grad_mixed[:, at])
                grad_probs = product_transposed(grad_mixed[:, at], made[:, value])
                delta = jnp.sum(probs * grad_probs, axis=1, keepdims=True)
                grad_scores = (probs * (grad_probs - delta)).astype(bf16)
                grad_query = product(grad_scores, made[:, key]) * HEAD_SIZE ** (-0.5)
                grad_made[:, at] = grad_query.astype(bf16)
                grad_key = grad_key + dot_rows(grad_scores, made[:, at]) * HEAD_SIZE ** (-0.5)
            grad_made[:, key] = grad_key.astype(bf16)
            grad_made[:, value] = grad_value.astype(bf16)
        grads[...] = dot_rows(normed[...], grad_made[...]).astype(bf16)
        block_copies(order, grads, (near, far), sems, False)
        block_waits(grads, (near, far), sems, False)

    return pl.pallas_call(
        kernel,
        in_specs=[scalars, scalars] + [in_vmem] * 4,
        out_specs=[in_vmem, anywhere, anywhere],
        out_shape=[jax.ShapeDtypeStruct((total, columns), bf16)]
        + half_shapes(places, width, columns),
        scratch_shapes=[
            pltpu.VMEM((width, columns), bf16),
            pltpu.SemaphoreType.DMA((places,)),
        ],
        compiler_params=room,
        cost_estimate=no_cost,
    )(order, spot, grad_mixed, normed, made, logs)


def normed_back(order, grad_made, halves):
    total, columns = grad_made.shape
    width = 2 * halves[0].shape[0] * halves[0].shape[1]
    rows = total // 2

    def kernel(order, grad_made, near, far, own, other, weight, sems):
        block_copies(order, weight, (near, far), sems, True)
        block_waits(weight, (near, far), sems, True)
        other[...] = product_transposed(grad_made[pl.ds(rows, rows), :], weight[...]).astype(bf16)
        own[...] = product_transposed(grad_made[pl.ds(0, rows), :], weight[...])

    return pl.pallas_call(
        kernel,
        in_specs=[scalars, in_vmem, anywhere, anywhere],
        out_specs=[in_vmem] * 2,
        out_shape=[
            jax.ShapeDtypeStruct((rows, width), f32),
            jax.ShapeDtypeStruct((rows, width), bf16),
        ],
        scratch_shapes=[
            pltpu.VMEM((width, columns), bf16),
            pltpu.SemaphoreType.DMA((2 * halves[0].shape[0],)),
        ],
        compiler_params=room,
        cost_estimate=no_cost,
    )(order, grad_made, *halves)


class Experts:
    def __init__(self, held, cores, groups, rows, capacity):
        self.held, self.cores, self.groups = held, cores, groups
        self.rows, self.capacity = rows, capacity

    def fetch(self, spots, shares, weight, sems, k):
        return [
            pltpu.make_async_copy(
                shares.at[spots[k, c]], weight.at[k % 2, c], sems.at[k % 2, c]
            )
            for c in range(self.cores)
        ]

    def weights_of(self, step, spots, shares, weight, sems):
        for k in range(self.held):

            @pl.when(step == k)
            def _():
                if k == 0:
                    for copy in self.fetch(spots, shares, weight, sems, 0):
                        copy.start()
                if k + 1 < self.held:
                    for copy in self.fetch(spots, shares, weight, sems, k + 1):
                        copy.start()

    def wait_weights(self, step, spots, shares, weight, sems):
        for k in range(self.held):

            @pl.when(step == k)
            def _():
                for copy in self.fetch(spots, shares, weight, sems, k):
                    copy.wait()

    def taken(self, position, k, g):
        return slot_matrix(position[k, g : g + 1, :], self.capacity)

    def dispatch(self, position, tokens, into):
        for g in range(self.groups):
            found = [self.taken(position, k, g).astype(bf16) for k in range(self.held)]
            found = jnp.concatenate(found, axis=0)
            found = product(found, tokens[pl.ds(g * self.rows, self.rows), :]).astype(bf16)
            for k in range(self.held):
                part = found[k * self.capacity : (k + 1) * self.capacity]
                into[k, pl.ds(g * self.capacity, self.capacity), :] = part

    def scales(self, position, gate, step):
        columns = []
        for g in range(self.groups):
            taken = slot_matrix(position[step, pl.ds(g, 1), :], self.capacity)
            gates = jnp.where(taken, gate[step, pl.ds(g, 1), :], 0.0)
            columns.append(jnp.sum(gates, axis=1, keepdims=True))
        return jnp.concatenate(columns, axis=0)

    def keep(self, made, step, into):
        for g in range(self.groups):
            part = made[g * self.capacity : (g + 1) * self.capacity]
            at = pl.ds(pl.multiple_of(step * self.capacity, self.capacity), self.capacity)
            into[g, at, :] = part

    def combine(self, position, made, init, slots, sems, write):
        def start(g):
            return pltpu.make_async_copy(init.at[g], slots.at[g % 2], sems.at[g % 2])

        start(0).start()
        for g in range(self.groups):
            if g + 1 < self.groups:
                start(g + 1).start()
            found = [self.taken(position, k, g).astype(bf16) for k in range(self.held)]
            found = dot_rows(jnp.concatenate(found, axis=0), made[g])
            start(g).wait()
            write(g, found + slots[g % 2])


def experts_forward(position, gate, spots, capacity, tokens, shares, init):
    (held, groups, rows), (_, _, width, hidden) = position.shape, shares.shape
    cores, slots = spots.shape[1], groups * capacity
    plan = Experts(held, cores, groups, rows, capacity)

    def kernel(spots, position, gate, tokens, shares, init, out, work, pre, weight, rows_all, made, sums, sems, sum_sems):
        step = pl.program_id(0)
        plan.weights_of(step, spots, shares, weight, sems)

        @pl.when(step == 0)
        def _():
            plan.dispatch(position, tokens, rows_all)

        plan.wait_weights(step, spots, shares, weight, sems)
        slot = lax.rem(step, 2)
        mine = rows_all[step]
        work[0] = mine
        produced = 0.0
        for c in range(cores):
            pre_gate = product(mine, weight[slot, c, 0])
            pre_up = product(mine, weight[slot, c, 1])
            pre[0, c, 0], pre[0, c, 1] = pre_gate, pre_up
            act = (pre_gate * (1.0 / (1.0 + jnp.exp(-pre_gate))) * pre_up).astype(bf16)
            produced = produced + product_transposed(act, weight[slot, c, 2])
        plan.keep((produced * plan.scales(position, gate, step)).astype(bf16), step, made)

        @pl.when(step == held - 1)
        def _():
            def write(g, total):
                out[g] = total.astype(bf16)

            plan.combine(position, made, init, sums, sum_sems, write)

    whole = pl.BlockSpec(position.shape, lambda j: (0, 0, 0))
    return pl.pallas_call(
        kernel,
        grid=(held,),
        in_specs=[
            scalars,
            whole,
            whole,
            pl.BlockSpec(tokens.shape, lambda j: (0, 0), pipeline_mode=pl.Buffered(1)),
            anywhere,
            anywhere,
        ],
        out_specs=[
            pl.BlockSpec((groups, rows, width), lambda j: (0, 0, 0)),
            pl.BlockSpec((1, slots, width), lambda j: (j, 0, 0)),
            pl.BlockSpec((1, cores, 2, slots, hidden), lambda j: (j, 0, 0, 0, 0)),
        ],
        out_shape=[
            jax.ShapeDtypeStruct((groups, rows, width), bf16),
            jax.ShapeDtypeStruct((held, slots, width), bf16),
            jax.ShapeDtypeStruct((held, cores, 2, slots, hidden), f32),
        ],
        scratch_shapes=[
            pltpu.VMEM((2, cores, 3, width, hidden), bf16),
            pltpu.VMEM((held, slots, width), bf16),
            pltpu.VMEM((groups, held * capacity, width), bf16),
            pltpu.VMEM((2, rows, width), f32),
            pltpu.SemaphoreType.DMA((2, cores)),
            pltpu.SemaphoreType.DMA((2,)),
        ],
        compiler_params=room,
        cost_estimate=no_cost,
    )(spots, position, gate, tokens, shares, init.reshape(groups, rows, width))


def experts_backward(position, gate, spots, capacity, tokens, work, pre, shares, init):
    (held, groups, rows), (_, _, width, hidden) = position.shape, shares.shape
    cores, slots = spots.shape[1], groups * capacity
    plan = Experts(held, cores, groups, rows, capacity)

    def kernel(
        spots, position, gate, tokens, work, pre, shares, init, out, grads, weight, rows_all, made, sums, fresh,
        found, sems, sum_sems, out_sems,
    ):
        step = pl.program_id(0)
        plan.weights_of(step, spots, shares, weight, sems)

        @pl.when(step == 0)
        def _():
            plan.dispatch(position, tokens, rows_all)

        plan.wait_weights(step, spots, shares, weight, sems)
        slot = lax.rem(step, 2)
        scale = plan.scales(position, gate, step)
        mine, produced, chosen, acts, pres = rows_all[step], 0.0, 0.0, [], []
        for c in range(cores):
            back = product(mine, weight[slot, c, 2])
            pre_gate, pre_up = pre[0, c, 0], pre[0, c, 1]
            logistic = 1.0 / (1.0 + jnp.exp(-pre_gate))
            activated = pre_gate * logistic * pre_up
            chosen = chosen + jnp.sum(back * activated, axis=1, keepdims=True)
            acts.append((activated * scale).astype(bf16))
            back = back * scale
            grad_gate = back * pre_up * logistic * (1.0 + pre_gate * (1.0 - logistic))
            pres.append((grad_gate.astype(bf16), (back * pre_gate * logistic).astype(bf16)))
            for s in range(2):
                produced = produced + product_transposed(pres[c][s], weight[slot, c, s])
        plan.keep(produced.astype(bf16), step, made)
        for g in range(groups):
            taken = slot_matrix(position[step, pl.ds(g, 1), :], capacity)
            part = chosen[g * capacity : (g + 1) * capacity]
            found[step, pl.ds(g, 1), :] = jnp.sum(jnp.where(taken, part, 0.0), axis=0, keepdims=True)

        def store(k):
            return [
                pltpu.make_async_copy(fresh.at[c], grads.at[spots[k, c]], out_sems.at[c])
                for c in range(cores)
            ]

        for k in range(1, held):

            @pl.when(step == k)
            def _():
                for copy in store(k - 1):
                    copy.wait()

        for c in range(cores):
            both = dot_rows(work[0], jnp.concatenate(pres[c], axis=1)).astype(bf16)
            fresh[c, 0], fresh[c, 1] = both[:, :hidden], both[:, hidden:]
        both = dot_rows(mine, jnp.concatenate(acts, axis=1)).astype(bf16)
        for c in range(cores):
            fresh[c, 2] = both[:, c * hidden : (c + 1) * hidden]
        for k in range(held):

            @pl.when(step == k)
            def _():
                for copy in store(k):
                    copy.start()

        @pl.when(step == held - 1)
        def _():
            def write(g, total):
                out[g, pl.ds(0, rows), :] = total.astype(bf16)
                tail = jnp.concatenate([found[k, g : g + 1, :] for k in range(held)], axis=0)
                high = tail.astype(bf16).astype(f32)
                tail = [high, tail - high, jnp.zeros((TAIL - 2 * held, rows), f32)]
                out[g, pl.ds(rows, TAIL), pl.ds(0, rows)] = jnp.concatenate(tail, axis=0).astype(bf16)

            plan.combine(position, made, init, sums, sum_sems, write)
            for copy in store(held - 1):
                copy.wait()

    whole = pl.BlockSpec(position.shape, lambda j: (0, 0, 0))
    return pl.pallas_call(
        kernel,
        grid=(held,),
        in_specs=[
            scalars,
            whole,
            whole,
            pl.BlockSpec(tokens.shape, lambda j: (0, 0), pipeline_mode=pl.Buffered(1)),
            pl.BlockSpec((1, slots, width), lambda j: (j, 0, 0)),
            pl.BlockSpec((1, cores, 2, slots, hidden), lambda j: (j, 0, 0, 0, 0)),
            anywhere,
            anywhere,
        ],
        out_specs=[pl.BlockSpec((groups, rows + TAIL, width), lambda j: (0, 0, 0)), anywhere],
        out_shape=[
            jax.ShapeDtypeStruct((groups, rows + TAIL, width), bf16),
            jax.ShapeDtypeStruct(shares.shape, bf16),
        ],
        scratch_shapes=[
            pltpu.VMEM((2, cores, 3, width, hidden), bf16),
            pltpu.VMEM((held, slots, width), bf16),
            pltpu.VMEM((groups, held * capacity, width), bf16),
            pltpu.VMEM((2, rows, width), f32),
            pltpu.VMEM((cores, 3, width, hidden), bf16),
            pltpu.VMEM(position.shape, f32),
            pltpu.SemaphoreType.DMA((2, cores)),
            pltpu.SemaphoreType.DMA((2,)),
            pltpu.SemaphoreType.DMA((cores,)),
        ],
        compiler_params=room,
        cost_estimate=no_cost,
    )(spots, position, gate, tokens, work, pre, shares, init.reshape(groups, rows, width))


def spread_shared(lay, shared_in, shared_out, member):
    rows, hidden = shared_out.shape
    part = hidden // len(lay.g_masks)
    stacked = jnp.concatenate([shared_in, shared_out[None]], axis=0)
    stacked = stacked.reshape(3 * rows, hidden)
    member_rows = member.reshape(-1, part)

    def piece(mask):
        chunk = lax.dynamic_slice_in_dim(stacked, lay.chunk(mask) * part, part, 1)
        return jnp.concatenate([chunk, member_rows], axis=0)

    pieces = [piece(0)] + [lay.shift(piece(m), m) for m in lay.g_masks[1:]]
    chunks = jnp.stack([p[: 3 * rows].reshape(3, rows, part) for p in pieces])
    return chunks, jnp.stack([p[3 * rows :].reshape(member.shape) for p in pieces])


def gather_shared(lay, blocks):
    _, _, matrices, rows, part = (len(blocks),) + blocks[0].shape
    everyone = jnp.stack(blocks, axis=1)
    natural = everyone.reshape((lay.dp, matrices, rows, part))[lay.rows_order()]
    return natural.transpose(1, 0, 2, 3).reshape(matrices, lay.dp * rows, part)


def scatter_shared(lay, grads, after):
    part = grads.shape[2] // lay.tp
    rows = grads.shape[1] // lay.dp
    own = lay.scatter_core([grads[:, :, k * part : (k + 1) * part] for k in range(lay.tp)])
    natural = own.astype(bf16).reshape(3, lay.dp, rows, part).transpose(1, 0, 2, 3)
    blocks = natural[lay.rows_apart()].reshape(len(lay.g_masks), len(lay.w_masks), 3, rows, part)
    summed = lay.scatter_w([blocks[:, k] for k in range(len(lay.w_masks))], after[0])
    summed = behind(summed, after[2])
    out = jnp.zeros((3, rows, part * len(lay.g_masks)), f32)
    for k, mask in enumerate(lay.g_masks):
        got = summed[k] if k == 0 else lay.shift(summed[k].astype(bf16), mask).astype(f32)
        out = lax.dynamic_update_slice_in_dim(out, got, lay.chunk(mask) * part, 2)
    return out


def scatter_parts(lay, parts):
    return [lay.shift(part, mask) if mask else part for part, mask in zip(parts, lay.g_masks)]


def on_device(
    block_input,
    teacher,
    lengths,
    routes,
    gain_attn,
    w_query,
    key_value_weight,
    w_out,
    gain_moe,
    w_router,
    w_shared_in,
    w_shared_out,
    w_expert_in,
    w_expert_out,
):
    lay = Layout()
    own_rows, width = block_input.shape
    tp, dp = lay.tp, lay.dp
    sequence_length = own_rows * tp
    experts = w_expert_in.shape[0] * dp
    capacity = max(2, own_rows * TOPK * 4 // (3 * experts))
    n_g, n_w = len(lay.g_masks), len(lay.w_masks)
    length = lengths[lay.place]
    slices = jnp.array(range(tp), jnp.int32) ^ lay.core
    positions = (slices[:, None] * own_rows + jnp.arange(own_rows)[None, :]).reshape(-1)
    own_valid = (positions[:own_rows] < length).astype(f32)[:, None]
    head_count = w_query.shape[1] // HEAD_SIZE
    kv_count = key_value_weight.shape[2] // HEAD_SIZE
    head_group = head_count // kv_count
    q_dim, kv_dim = head_count * HEAD_SIZE, kv_count * HEAD_SIZE
    in_kernel = n_g * own_rows <= 1024
    forward = experts_forward if in_kernel else experts_forward_plain
    backward = experts_backward if in_kernel else experts_backward_plain

    own_routes = lax.dynamic_slice_in_dim(routes, lay.core * own_rows, own_rows, 0)
    expert_ids = jnp.arange(experts, dtype=jnp.int32)
    member = jnp.any(own_routes.T[None, :, :] == expert_ids[:, None, None], axis=1)
    held_ids = lay.place ^ jnp.array(lay.w_masks, jnp.int32)
    held_hot = (held_ids[:, None] == expert_ids).astype(f32)
    shared_parts, group_member = spread_shared(
        lay, w_shared_in, w_shared_out, member.astype(bf16)
    )
    held_member = contract("je,get->jgt", held_hot.astype(bf16), group_member)
    before = jnp.triu(jnp.ones((own_rows, own_rows), bf16), 1)
    position = contract("jgu,ut->jgt", held_member.astype(bf16), before)
    position = jnp.where(held_member > 0, position, -1.0)

    near, far = (1 << bit for bit in lay.w_bits)
    input_slices = lay.gather_core(block_input)
    qkv = Tree(lay, jnp.concatenate([w_query, key_value_weight[0], key_value_weight[1]], axis=1))
    router_pad = jnp.zeros((w_router.shape[0], -experts % 128), bf16)
    out = Tree(lay, jnp.concatenate([w_out, w_router, router_pad], axis=1))
    steps = len(lay.tree_bits)
    qkv.step()
    out.step(qkv.marks[0])
    qkv.step(shared_parts, input_slices, group_member)
    out.step(qkv.marks[1])
    for k in range(2, steps):
        qkv.step(out.marks[k - 2])
        out.step(qkv.marks[k])
    expert_shares = lax.all_gather(
        behind(jnp.concatenate([w_expert_in[0], w_expert_out], axis=0), qkv.marks[2]),
        ("dp", "tensor"),
        axis_index_groups=lay.w_groups(),
    )
    shared_far = lay.shift(behind(shared_parts, qkv.marks[-2], out.marks[1]), far)
    shared_near = lay.shift(behind(jnp.stack([shared_parts, shared_far]), out.marks[-2]), near)

    spot = jnp.stack([lay.core, length]).astype(jnp.int32)
    in_order = lay.tree_order()
    residual = block_input.astype(f32)
    _, scale_attn = normalize_rows(residual, gain_attn)

    def by_core(rows):
        return [rows[k * own_rows : (k + 1) * own_rows] for k in range(tp)]

    if in_kernel:
        normed_all, projected, mixed_heads, logs = attend(
            in_order, spot, *input_slices, gain_attn, qkv.halves, head_count, kv_count
        )
        *attn_parts, out_router = project_out(
            in_order, mixed_heads, out.halves
        )
    else:
        qkv_full, out_router = lay.in_order(qkv.halves), lay.in_order(out.halves)
        normed_all, _ = normalize_rows(
            jnp.concatenate(input_slices, axis=0).astype(f32), gain_attn
        )
        projected = product(normed_all, qkv_full).astype(bf16)
        queries = projected[:, :q_dim].reshape(sequence_length, kv_count, head_group, HEAD_SIZE)
        key_row_table = projected[:, q_dim : q_dim + kv_dim].reshape(
            sequence_length, kv_count, HEAD_SIZE
        )
        value_row_table = projected[:, q_dim + kv_dim :].reshape(
            sequence_length, kv_count, HEAD_SIZE
        )
        allowed = (positions[None, :] <= positions[:, None]) & (positions[None, :] < length)
        scores = contract("qvgd,kvd->vgqk", queries, key_row_table) * HEAD_SIZE ** (-0.5)
        scores = jnp.where(allowed, scores, masked_score)
        row_max = jnp.max(scores, axis=-1, keepdims=True)
        exponent_terms = jnp.exp(scores - row_max)
        row_sum = jnp.sum(exponent_terms, axis=-1, keepdims=True)
        probs_full = exponent_terms / row_sum
        probs_low = probs_full.astype(bf16)
        mixed_heads = (
            contract("vgqk,kvd->qvgd", probs_low, value_row_table)
            .astype(bf16)
            .reshape(sequence_length, q_dim)
        )
        attn_parts = by_core(product_transposed(mixed_heads, out_router[:, :q_dim]))
    router_full = out_router[:, q_dim : q_dim + experts]
    hidden = residual + lay.scatter_core(attn_parts)
    moe_own, scale_moe = normalize_rows(hidden, gain_moe)

    arrived = lay.gather_g(moe_own)
    shared_own = gather_shared(lay, [shared_parts, shared_near[0], shared_far, shared_near[1]])
    shared_full = jnp.concatenate(lay.gather_core(shared_own), axis=2)
    shared_in_full, shared_out_full = shared_full[:2], shared_full[2]

    group_rows = jnp.concatenate(arrived, axis=0)
    logits = lax.dot_general(
        router_full, group_rows, (((0,), (1,)), ((), ())), preferred_element_type=f32
    )
    shown = jnp.where(
        group_member.transpose(1, 0, 2).reshape(experts, -1) > 0, logits, masked_score
    )
    gate_terms = jnp.exp(shown - jnp.max(shown, axis=0, keepdims=True))
    gates = gate_terms / jnp.sum(gate_terms, axis=0, keepdims=True)
    own_gates = gates[:, :own_rows]
    held_gates = jnp.sum(held_hot[:, :, None] * gates[None], axis=1).reshape(n_w, n_g, own_rows)
    shared_pre = contract("td,cdf->ctf", group_rows, shared_in_full)
    shared_act = (jax.nn.silu(shared_pre[0]) * shared_pre[1]).astype(bf16)
    total = product_transposed(shared_act, shared_out_full)
    spots = lay.w_spots()
    total, work, pre = forward(
        position, held_gates, spots, capacity, group_rows, expert_shares, total
    )

    def scatter_g(parts):
        return sum(part.astype(f32) for part in scatter_parts(lay, parts))

    out_rows = (hidden + scatter_g([total[k] for k in range(n_g)])) * own_valid
    residual_error = (out_rows - teacher.astype(f32)) * own_valid
    loss_part = 0.5 * jnp.sum(residual_error * residual_error)

    group_grad = jnp.concatenate(lay.gather_g(residual_error.astype(bf16)), axis=0)
    grad_shared_act = product(group_grad, shared_out_full)
    grad_shared_out = product_left(group_grad, shared_act)
    grad_shared_pre = jnp.stack(swish_back(shared_pre[0], shared_pre[1], grad_shared_act))
    grad_shared_in = contract("td,ctf->cdf", group_rows, grad_shared_pre)
    total = contract("ctf,cdf->td", grad_shared_pre, shared_in_full)
    total, grad_shares = backward(
        position, held_gates, spots, capacity, group_grad, work, pre, expert_shares, total
    )
    grad_expert = lax.psum_scatter(
        grad_shares, ("dp", "tensor"), axis_index_groups=lay.w_groups()
    ).astype(f32)
    received = scatter_parts(lay, [total[k] for k in range(n_g)])
    returned = received[0][:own_rows].astype(f32)
    for part in received[1:]:
        returned = returned + part[:own_rows].astype(f32)
    gate_rows = [part[own_rows:, :own_rows].astype(f32) for part in received]
    gate_rows = [rows[:n_w] + rows[n_w : 2 * n_w] for rows in gate_rows]
    ids = lay.place ^ jnp.array([g ^ w for g in lay.g_masks for w in lay.w_masks], jnp.int32)
    placed = (expert_ids[:, None] == ids).astype(f32)[:, :, None]
    grad_gates = jnp.sum(placed * jnp.concatenate(gate_rows, axis=0)[None], axis=1)
    grad_logits = (
        own_gates * (grad_gates - jnp.sum(own_gates * grad_gates, axis=0, keepdims=True))
    ).astype(bf16)
    grad_router_part = lax.dot_general(
        moe_own, grad_logits, (((0,), (1,)), ((), ())), preferred_element_type=f32
    )
    grad_normed_own = returned + lax.dot_general(
        grad_logits, router_full, (((0,), (1,)), ((), ())), preferred_element_type=f32
    )

    grad_from_moe, grad_gain_moe_part = normalize_back(hidden, scale_moe, gain_moe, grad_normed_own)
    grad_hidden = residual_error + grad_from_moe
    grad_slices = lay.gather_core(grad_hidden.astype(bf16))
    grad_router_part = jnp.pad(
        lay.scatter_core([grad_router_part] * tp).astype(bf16), ((0, 0), (0, -experts % 128))
    )
    if in_kernel:
        grad_mixed, *out_back_halves = project_out_back(
            lay.tree_order(), *grad_slices, out_router, mixed_heads, grad_router_part
        )
        grad_projected, *qkv_back_halves = attend_back(
            lay.tree_order(), spot, grad_mixed, normed_all, projected, logs, head_count, kv_count
        )
        normed_parts = normed_back(in_order, grad_projected, qkv.halves)
    else:
        grad_attn = jnp.concatenate(grad_slices, axis=0)
        grad_mixed = (
            product(grad_attn, out_router[:, :q_dim])
            .astype(bf16)
            .reshape(sequence_length, kv_count, head_group, HEAD_SIZE)
        )
        grad_values = contract("vgqk,qvgd->kvd", probs_low, grad_mixed)
        grad_probs = contract("qvgd,kvd->vgqk", grad_mixed, value_row_table)
        delta_sum = jnp.sum(probs_full * grad_probs, axis=-1, keepdims=True)
        grad_scores = (probs_full * (grad_probs - delta_sum)).astype(bf16)
        grad_queries = contract("vgqk,kvd->qvgd", grad_scores, key_row_table) * HEAD_SIZE ** (-0.5)
        grad_keys = contract("vgqk,qvgd->kvd", grad_scores, queries) * HEAD_SIZE ** (-0.5)
        grad_projected = jnp.concatenate(
            [
                grad_queries.astype(bf16).reshape(sequence_length, q_dim),
                grad_keys.astype(bf16).reshape(sequence_length, kv_dim),
                grad_values.astype(bf16).reshape(sequence_length, kv_dim),
            ],
            axis=1,
        )
        out_back_halves = lay.in_halves(
            jnp.concatenate([product_left(grad_attn, mixed_heads).astype(bf16), grad_router_part], axis=1)
        )
        qkv_back_halves = lay.in_halves(product_left(normed_all, grad_projected))
        normed_parts = by_core(product_transposed(grad_projected, qkv_full))
    out_back = Sum(lay, out_back_halves)
    keep, send = qkv_back_halves
    send = behind(send, out_back.step(grad_projected))
    qkv_back = Sum(lay, (keep, send))
    qkv_back.step()
    for k in range(1, steps):
        out_back.step(qkv_back.marks[k - 1] if k > 1 else grad_projected)
        qkv_back.step()
    grad_qkv, grad_out_router = qkv_back.total[0], out_back.total[0]
    qkv_back = qkv_back.marks
    grad_normed_attn = lay.scatter_core(normed_parts)
    grad_from_attn, grad_gain_attn_part = normalize_back(
        residual, scale_attn, gain_attn, grad_normed_attn
    )
    input_grad = grad_hidden + grad_from_attn
    grad_w_kv = jnp.stack(
        [grad_qkv[:, q_dim : q_dim + kv_dim], grad_qkv[:, q_dim + kv_dim :]], axis=0
    )
    small = jnp.stack(
        [grad_gain_attn_part, grad_gain_moe_part, jnp.full((width,), loss_part, f32)], axis=0
    )
    small = lay.sum_all(small, qkv_back)
    loss = small[2, 0] / (jnp.sum(lengths).astype(f32) * width)
    grad_shared = scatter_shared(
        lay, jnp.concatenate([grad_shared_in, grad_shared_out[None]]), qkv_back
    )
    return (
        out_rows.astype(bf16),
        loss,
        input_grad,
        small[0],
        grad_qkv[:, :q_dim],
        grad_w_kv,
        grad_out_router[:, :q_dim],
        small[1],
        grad_out_router[:, q_dim : q_dim + experts],
        grad_shared[:2],
        grad_shared[2],
        grad_expert[None, :2],
        grad_expert[2:],
    )


def solution(mesh):
    rows, weights = P(("dp", "tensor"), None), P("dp", "tensor")
    stacked = P(None, "dp", "tensor")
    expert_in, expert_out = P("dp", None, None, "tensor"), P("dp", None, "tensor")
    return jax.shard_map(
        on_device,
        mesh=mesh,
        in_specs=(
            rows,
            rows,
            P(),
            P("dp", None),
            P(),
            weights,
            stacked,
            weights,
            P(),
            P("dp", None),
            stacked,
            weights,
            expert_in,
            expert_out,
        ),
        out_specs=(
            rows,
            P(),
            rows,
            P(),
            weights,
            stacked,
            weights,
            P(),
            P("dp", None),
            stacked,
            weights,
            expert_in,
            expert_out,
        ),
        check_vma=False,
    )
```

```python
import jax
import jax.numpy as jnp
from jax import lax
from jax.experimental import pallas as pl
from jax.experimental.pallas import tpu as pltpu
from jax.sharding import PartitionSpec as P

HEAD_SIZE = 128
TOPK = 6

norm_eps = 1e-05
masked_score = -1e30
TAIL = 16
bf16 = jnp.bfloat16
f32 = jnp.float32


def product(left_side, right_side):
    return jnp.dot(left_side, right_side, preferred_element_type=f32)


def product_transposed(left_side, right_side):
    return lax.dot_general(
        left_side, right_side, (((1,), (1,)), ((), ())), preferred_element_type=f32
    )


def product_left(left_side, right_side):
    return lax.dot_general(
        left_side, right_side, (((0,), (0,)), ((), ())), preferred_element_type=f32
    )


def contract(spec, *operands):
    return jnp.einsum(spec, *operands, preferred_element_type=f32)


def normalize_rows(values, gain):
    row_scale = lax.rsqrt(jnp.mean(values * values, axis=-1, keepdims=True) + norm_eps)
    return ((values * row_scale * gain).astype(bf16), row_scale)


def normalize_back(values, row_scale, gain, grad_normed):
    scaled = grad_normed * gain
    inner_mean = jnp.mean(scaled * values, axis=-1, keepdims=True)
    grad_values = row_scale * (scaled - values * row_scale * row_scale * inner_mean)
    grad_gain = jnp.sum(grad_normed * values * row_scale, axis=0)
    return (grad_values, grad_gain)


def swish_back(pre_gate, pre_up, grad_act):
    logistic = jax.nn.sigmoid(pre_gate)
    grad_gate = grad_act * pre_up * logistic * (1.0 + pre_gate * (1.0 - logistic))
    grad_up = grad_act * pre_gate * logistic
    return grad_gate.astype(bf16), grad_up.astype(bf16)


def subset_masks(bits):
    masks = [0]
    for bit in bits:
        masks = masks + [mask | (1 << bit) for mask in masks]
    return masks


def behind(values, *others):
    return lax.optimization_barrier((values,) + others)[0]


class Tree:
    def __init__(self, lay, shard):
        self.lay, self.halves, self.marks = lay, (shard[None],), []

    def step(self, *others):
        held = jnp.concatenate(self.halves, axis=0)
        if others:
            held = behind(held, *others)
        self.marks.append(self.lay.shift(held, 1 << self.lay.tree_bits[len(self.marks)]))
        self.halves = (held, self.marks[-1])
        return self.marks[-1]


class Sum:
    def __init__(self, lay, halves):
        self.lay, (self.keep, self.send), self.marks = lay, halves, []

    def step(self, *others):
        got = self.lay.shift(self.send, 1 << self.lay.tree_bits[-1 - len(self.marks)])
        if others:
            got = behind(got, *others)
        self.marks.append(got)
        self.total = self.keep.astype(f32) + got.astype(f32)
        half = self.total.shape[0] // 2
        self.keep, self.send = self.total[:half], self.total[half:].astype(bf16)
        return got


class Layout:
    def __init__(self):
        self.dp = lax.axis_size("dp")
        self.tp = lax.axis_size("tensor")
        self.place = lax.axis_index("dp")
        self.core = lax.axis_index("tensor")
        bits = self.dp.bit_length() - 1
        self.w_bits = [bit for bit in (1, 3) if bit < bits]
        self.g_bits = [bit for bit in range(bits) if bit not in self.w_bits]
        self.w_masks = subset_masks(self.w_bits)
        self.g_masks = subset_masks(self.g_bits)
        self.tree_bits = list(range(bits - 1, -1, -1))

    def shift(self, values, mask):
        return lax.ppermute(values, "dp", [(i, i ^ mask) for i in range(self.dp)])

    def w_groups(self):
        groups = []
        for i in range(self.dp):
            if all(i & mask == 0 for mask in self.w_masks):
                places = sorted(i ^ mask for mask in self.w_masks)
                groups.append([place * self.tp + c for place in places for c in range(self.tp)])
        return groups

    def w_spots(self):
        bits = [(self.place >> bit) & 1 for bit in self.w_bits]
        rows = []
        for k in range(len(self.w_masks)):
            spot = sum((bit ^ ((k >> n) & 1)) << n for n, bit in enumerate(bits))
            rows.append(jnp.stack([spot * self.tp + (self.core ^ c) for c in range(self.tp)]))
        return jnp.stack(rows).astype(jnp.int32)

    def shift_core(self, values, mask):
        return lax.ppermute(values, "tensor", [(i, i ^ mask) for i in range(self.tp)])

    def tree_order(self):
        apart = self.place ^ jnp.arange(self.dp)
        return sum(((apart >> bit) & 1) << k for k, bit in enumerate(self.tree_bits))

    def in_order(self, halves):
        whole = jnp.concatenate(halves, axis=0)[self.tree_order()]
        return whole.reshape((-1,) + whole.shape[2:])

    def in_halves(self, whole):
        blocks = whole.astype(bf16).reshape((self.dp, -1) + whole.shape[1:])
        rel = jnp.arange(self.dp)
        apart = sum(((rel >> k) & 1) << bit for k, bit in enumerate(self.tree_bits))
        at = self.place ^ apart
        return blocks[at[: self.dp // 2]], blocks[at[self.dp // 2 :]]

    def gather_g(self, values):
        return [values] + [self.shift(values, mask) for mask in self.g_masks[1:]]

    def scatter_w(self, blocks, after):
        near, far = (1 << bit for bit in self.w_bits)
        both = jnp.stack([blocks[3], blocks[1]]).astype(bf16)
        far_one, own = behind(self.shift(both, near), after)
        far_one = self.shift((blocks[2].astype(f32) + far_one.astype(f32)).astype(bf16), far)
        return blocks[0].astype(f32) + own.astype(f32) + far_one.astype(f32)

    def gather_core(self, values):
        return [values] + [self.shift_core(values, k) for k in range(1, self.tp)]

    def scatter_core(self, blocks):
        total = blocks[0].astype(f32)
        for k in range(1, self.tp):
            total = total + self.shift_core(blocks[k].astype(bf16), k).astype(f32)
        return total

    def sum_all(self, values, marks):
        for bit, mark in enumerate(marks):
            values = behind(values, mark)
            values = values + self.shift(values, 1 << bit)
        for bit in range(self.tp.bit_length() - 1):
            values = values + self.shift_core(values, 1 << bit)
        return values

    def chunk(self, mask):
        place = self.place ^ mask
        return sum(((place >> bit) & 1) << k for k, bit in enumerate(self.g_bits))

    def rows_order(self):
        apart = self.place ^ jnp.arange(self.dp)
        g = sum(((apart >> bit) & 1) << k for k, bit in enumerate(self.g_bits))
        w = sum(((apart >> bit) & 1) << k for k, bit in enumerate(self.w_bits))
        return g * len(self.w_masks) + w

    def rows_apart(self):
        masks = jnp.array([g | w for g in self.g_masks for w in self.w_masks], jnp.int32)
        return self.place ^ masks


def slots_of(position, capacity):
    slots = jnp.arange(capacity, dtype=f32)[:, None]
    return (position[:, :, None, :] == slots).astype(bf16)


def experts_forward_plain(position, gate, spots, capacity, tokens, shares, init):
    (held, groups, rows), width = position.shape, tokens.shape[1]
    taken = slots_of(position, capacity)
    work = contract("jgct,gtd->jgcd", taken, tokens.reshape(groups, rows, width)).astype(bf16)
    work = work.reshape(held, groups * capacity, width)
    scale = jnp.sum(taken.astype(f32) * gate[:, :, None, :], axis=-1).reshape(held, -1, 1)
    pre, made = [], 0.0
    for c in range(spots.shape[1]):
        weight = shares[spots[:, c]]
        pre.append(contract("jrd,jsdf->jsrf", work, weight[:, :2]))
        act = (jax.nn.silu(pre[-1][:, 0]) * pre[-1][:, 1]).astype(bf16)
        made = made + contract("jrf,jdf->jrd", act, weight[:, 2])
    made = (made * scale).astype(bf16).reshape(held, groups, capacity, width)
    total = init.reshape(groups, rows, width) + contract("jgct,jgcd->gtd", taken, made)
    return total.astype(bf16), work, jnp.stack(pre, axis=1)


def experts_backward_plain(position, gate, spots, capacity, tokens, work, pre, shares, init):
    (held, groups, rows), width = position.shape, tokens.shape[1]
    taken = slots_of(position, capacity)
    grad_rows = contract("jgct,gtd->jgcd", taken, tokens.reshape(groups, rows, width)).astype(bf16)
    grad_rows = grad_rows.reshape(held, groups * capacity, width)
    scale = jnp.sum(taken.astype(f32) * gate[:, :, None, :], axis=-1).reshape(held, -1, 1)
    chosen, made, grads = 0.0, 0.0, jnp.zeros(shares.shape, bf16)
    for c in range(spots.shape[1]):
        weight = shares[spots[:, c]]
        back = contract("jrd,jdf->jrf", grad_rows, weight[:, 2])
        activated = jax.nn.silu(pre[:, c, 0]) * pre[:, c, 1]
        chosen = chosen + jnp.sum(back * activated, axis=-1)
        grad_pre = jnp.stack(swish_back(pre[:, c, 0], pre[:, c, 1], back * scale), axis=1)
        made = made + contract("jsrf,jsdf->jrd", grad_pre, weight[:, :2])
        grad_in = contract("jrd,jsrf->jsdf", work, grad_pre).astype(bf16)
        grad_out = contract("jrd,jrf->jdf", grad_rows, (activated * scale).astype(bf16)).astype(bf16)
        grads = grads.at[spots[:, c]].set(jnp.concatenate([grad_in, grad_out[:, None]], axis=1))
    made = made.astype(bf16).reshape(held, groups, capacity, width)
    total = init.reshape(groups, rows, width) + contract("jgct,jgcd->gtd", taken, made)
    chosen = jnp.sum(taken.astype(f32) * chosen.reshape(held, groups, capacity, 1), axis=2)
    tail = chosen.transpose(1, 0, 2)
    high = tail.astype(bf16).astype(f32)
    tail = jnp.concatenate([high, tail - high], axis=1)
    tail = jnp.pad(tail, ((0, 0), (0, TAIL - tail.shape[1]), (0, width - rows)))
    return jnp.concatenate([total, tail], axis=1).astype(bf16), grads


def dot_rows(left, right):
    return lax.dot_general(left, right, (((0,), (0,)), ((), ())), preferred_element_type=f32)


def slot_matrix(position, capacity):
    slots = lax.broadcasted_iota(jnp.int32, (capacity, position.shape[1]), 0).astype(f32)
    return slots == position


def block_copies(order, whole, halves, sems, inward):
    blocks, rows = halves[0].shape[0], halves[0].shape[1]
    for i in range(2 * blocks):
        part = whole.at[pl.ds(i * rows, rows)]
        for k, half in enumerate(halves):

            @pl.when((order[i] >= k * blocks) & (order[i] < (k + 1) * blocks))
            def _():
                block = half.at[order[i] - k * blocks]
                source, target = (block, part) if inward else (part, block)
                pltpu.make_async_copy(source, target, sems.at[i]).start()


def block_waits(whole, halves, sems, inward):
    blocks, rows = halves[0].shape[0], halves[0].shape[1]
    for i in range(2 * blocks):
        part = whole.at[pl.ds(i * rows, rows)]
        source, target = (halves[0].at[0], part) if inward else (part, halves[0].at[0])
        pltpu.make_async_copy(source, target, sems.at[i]).wait()


def score_mask(core, length, rows):
    row = lax.broadcasted_iota(jnp.int32, (rows, rows), 0)
    col = lax.broadcasted_iota(jnp.int32, (rows, rows), 1)
    first = core * (rows // 2)
    row = jnp.where(row < rows // 2, row + first, row - first)
    col = jnp.where(col < rows // 2, col + first, col - first)
    return (col <= row) & (col < length)


anywhere = pl.BlockSpec(memory_space=pl.ANY)
scalars = pl.BlockSpec(memory_space=pltpu.SMEM)
in_vmem = pl.BlockSpec(memory_space=pltpu.VMEM)
no_cost = pl.CostEstimate(flops=0, transcendentals=0, bytes_accessed=0)
room = pltpu.CompilerParams(vmem_limit_bytes=56 * 1024 * 1024)


def attend(order, spot, own, other, gain, halves, head_count, kv_count):
    rows, width = own.shape
    total, columns = 2 * rows, halves[0].shape[2]
    group = head_count // kv_count

    def kernel(order, spot, own, other, gain, near, far, normed, made, mixed, logs, weight, sems):
        block_copies(order, weight, (near, far), sems, True)
        for k, part in enumerate((own, other)):
            values = part[...].astype(f32)
            scale = lax.rsqrt(jnp.mean(values * values, axis=1, keepdims=True) + norm_eps)
            normed[pl.ds(k * rows, rows), :] = (values * scale * gain[...]).astype(bf16)
        block_waits(weight, (near, far), sems, True)
        made[...] = product(normed[...], weight[...]).astype(bf16)
        allowed = score_mask(spot[0], spot[1], total)
        for h in range(head_count):
            key = pl.ds((head_count + h // group) * HEAD_SIZE, HEAD_SIZE)
            value = pl.ds((head_count + kv_count + h // group) * HEAD_SIZE, HEAD_SIZE)
            at = pl.ds(h * HEAD_SIZE, HEAD_SIZE)
            scores = product_transposed(made[:, at], made[:, key]) * HEAD_SIZE ** (-0.5)
            scores = jnp.where(allowed, scores, masked_score)
            most = jnp.max(scores, axis=1, keepdims=True)
            terms = jnp.exp(scores - most)
            together = jnp.sum(terms, axis=1, keepdims=True)
            probs = (terms * (1.0 / together)).astype(bf16)
            mixed[:, at] = product(probs, made[:, value]).astype(bf16)
            logs[h] = most + jnp.log(together)

    return pl.pallas_call(
        kernel,
        in_specs=[scalars, scalars, in_vmem, in_vmem, in_vmem, anywhere, anywhere],
        out_specs=[in_vmem] * 4,
        out_shape=[
            jax.ShapeDtypeStruct((total, width), bf16),
            jax.ShapeDtypeStruct((total, columns), bf16),
            jax.ShapeDtypeStruct((total, head_count * HEAD_SIZE), bf16),
            jax.ShapeDtypeStruct((head_count, total, 1), f32),
        ],
        scratch_shapes=[
            pltpu.VMEM((width, columns), bf16),
            pltpu.SemaphoreType.DMA((2 * halves[0].shape[0],)),
        ],
        compiler_params=room,
        cost_estimate=no_cost,
    )(order, spot, own, other, gain[None], *halves)


def project_out(order, mixed, halves):
    total, columns = mixed.shape
    width = 2 * halves[0].shape[0] * halves[0].shape[1]
    rows = total // 2

    def kernel(order, mixed, near, far, own, other, weight, sems):
        block_copies(order, weight, (near, far), sems, True)
        block_waits(weight, (near, far), sems, True)
        other[...] = product_transposed(mixed[pl.ds(rows, rows), :], weight[:, :columns]).astype(bf16)
        own[...] = product_transposed(mixed[pl.ds(0, rows), :], weight[:, :columns])

    return pl.pallas_call(
        kernel,
        in_specs=[scalars, in_vmem, anywhere, anywhere],
        out_specs=[in_vmem] * 3,
        out_shape=[
            jax.ShapeDtypeStruct((rows, width), f32),
            jax.ShapeDtypeStruct((rows, width), bf16),
            jax.ShapeDtypeStruct((width, halves[0].shape[2]), bf16),
        ],
        scratch_shapes=[pltpu.SemaphoreType.DMA((2 * halves[0].shape[0],))],
        compiler_params=room,
        cost_estimate=no_cost,
    )(order, mixed, *halves)


def half_shapes(places, width, columns):
    block = jax.ShapeDtypeStruct((places // 2, width // places, columns), bf16)
    return [block, block]


def project_out_back(order, own, other, weight, mixed, router):
    total, columns = mixed.shape
    rows, width = own.shape
    places = order.shape[0]

    def kernel(order, own, other, weight, mixed, router, grad_mixed, near, far, grads, both, sems):
        both[pl.ds(0, rows), :] = own[...]
        both[pl.ds(rows, rows), :] = other[...]
        grads[:, :columns] = dot_rows(both[...], mixed[...]).astype(bf16)
        grads[:, columns:] = router[...]
        block_copies(order, grads, (near, far), sems, False)
        grad_mixed[...] = product(both[...], weight[:, :columns]).astype(bf16)
        block_waits(grads, (near, far), sems, False)

    return pl.pallas_call(
        kernel,
        in_specs=[scalars] + [in_vmem] * 5,
        out_specs=[in_vmem, anywhere, anywhere],
        out_shape=[jax.ShapeDtypeStruct((total, columns), bf16)]
        + half_shapes(places, width, weight.shape[1]),
        scratch_shapes=[
            pltpu.VMEM(weight.shape, bf16),
            pltpu.VMEM((total, width), bf16),
            pltpu.SemaphoreType.DMA((places,)),
        ],
        compiler_params=room,
        cost_estimate=no_cost,
    )(order, own, other, weight, mixed, router)


def attend_back(order, spot, grad_mixed, normed, made, logs, head_count, kv_count):
    total, width = normed.shape
    columns, group = made.shape[1], head_count // kv_count
    places = order.shape[0]

    def kernel(order, spot, grad_mixed, normed, made, logs, grad_made, near, far, grads, sems):
        allowed = score_mask(spot[0], spot[1], total)
        for v in range(kv_count):
            key = pl.ds((head_count + v) * HEAD_SIZE, HEAD_SIZE)
            value = pl.ds((head_count + kv_count + v) * HEAD_SIZE, HEAD_SIZE)
            grad_key, grad_value = 0.0, 0.0
            for h in range(v * group, (v + 1) * group):
                at = pl.ds(h * HEAD_SIZE, HEAD_SIZE)
                scores = product_transposed(made[:, at], made[:, key]) * HEAD_SIZE ** (-0.5)
                probs = jnp.where(allowed, jnp.exp(scores - logs[h]), 0.0)
                grad_value = grad_value + dot_rows(probs.astype(bf16), grad_mixed[:, at])
                grad_probs = product_transposed(grad_mixed[:, at], made[:, value])
                delta = jnp.sum(probs * grad_probs, axis=1, keepdims=True)
                grad_scores = (probs * (grad_probs - delta)).astype(bf16)
                grad_query = product(grad_scores, made[:, key]) * HEAD_SIZE ** (-0.5)
                grad_made[:, at] = grad_query.astype(bf16)
                grad_key = grad_key + dot_rows(grad_scores, made[:, at]) * HEAD_SIZE ** (-0.5)
            grad_made[:, key] = grad_key.astype(bf16)
            grad_made[:, value] = grad_value.astype(bf16)
        grads[...] = dot_rows(normed[...], grad_made[...]).astype(bf16)
        block_copies(order, grads, (near, far), sems, False)
        block_waits(grads, (near, far), sems, False)

    return pl.pallas_call(
        kernel,
        in_specs=[scalars, scalars] + [in_vmem] * 4,
        out_specs=[in_vmem, anywhere, anywhere],
        out_shape=[jax.ShapeDtypeStruct((total, columns), bf16)]
        + half_shapes(places, width, columns),
        scratch_shapes=[
            pltpu.VMEM((width, columns), bf16),
            pltpu.SemaphoreType.DMA((places,)),
        ],
        compiler_params=room,
        cost_estimate=no_cost,
    )(order, spot, grad_mixed, normed, made, logs)


def normed_back(order, grad_made, halves):
    total, columns = grad_made.shape
    width = 2 * halves[0].shape[0] * halves[0].shape[1]
    rows = total // 2

    def kernel(order, grad_made, near, far, own, other, weight, sems):
        block_copies(order, weight, (near, far), sems, True)
        block_waits(weight, (near, far), sems, True)
        other[...] = product_transposed(grad_made[pl.ds(rows, rows), :], weight[...]).astype(bf16)
        own[...] = product_transposed(grad_made[pl.ds(0, rows), :], weight[...])

    return pl.pallas_call(
        kernel,
        in_specs=[scalars, in_vmem, anywhere, anywhere],
        out_specs=[in_vmem] * 2,
        out_shape=[
            jax.ShapeDtypeStruct((rows, width), f32),
            jax.ShapeDtypeStruct((rows, width), bf16),
        ],
        scratch_shapes=[
            pltpu.VMEM((width, columns), bf16),
            pltpu.SemaphoreType.DMA((2 * halves[0].shape[0],)),
        ],
        compiler_params=room,
        cost_estimate=no_cost,
    )(order, grad_made, *halves)


class Experts:
    def __init__(self, held, cores, groups, rows, capacity):
        self.held, self.cores, self.groups = held, cores, groups
        self.rows, self.capacity = rows, capacity

    def fetch(self, spots, shares, weight, sems, k):
        return [
            pltpu.make_async_copy(
                shares.at[spots[k, c]], weight.at[k % 2, c], sems.at[k % 2, c]
            )
            for c in range(self.cores)
        ]

    def weights_of(self, step, spots, shares, weight, sems):
        for k in range(self.held):

            @pl.when(step == k)
            def _():
                if k == 0:
                    for copy in self.fetch(spots, shares, weight, sems, 0):
                        copy.start()
                if k + 1 < self.held:
                    for copy in self.fetch(spots, shares, weight, sems, k + 1):
                        copy.start()

    def wait_weights(self, step, spots, shares, weight, sems):
        for k in range(self.held):

            @pl.when(step == k)
            def _():
                for copy in self.fetch(spots, shares, weight, sems, k):
                    copy.wait()

    def taken(self, position, k, g):
        return slot_matrix(position[k, g : g + 1, :], self.capacity)

    def dispatch(self, position, tokens, into):
        for g in range(self.groups):
            found = [self.taken(position, k, g).astype(bf16) for k in range(self.held)]
            found = jnp.concatenate(found, axis=0)
            found = product(found, tokens[pl.ds(g * self.rows, self.rows), :]).astype(bf16)
            for k in range(self.held):
                part = found[k * self.capacity : (k + 1) * self.capacity]
                into[k, pl.ds(g * self.capacity, self.capacity), :] = part

    def scales(self, position, gate, step):
        columns = []
        for g in range(self.groups):
            taken = slot_matrix(position[step, pl.ds(g, 1), :], self.capacity)
            gates = jnp.where(taken, gate[step, pl.ds(g, 1), :], 0.0)
            columns.append(jnp.sum(gates, axis=1, keepdims=True))
        return jnp.concatenate(columns, axis=0)

    def keep(self, made, step, into):
        for g in range(self.groups):
            part = made[g * self.capacity : (g + 1) * self.capacity]
            at = pl.ds(pl.multiple_of(step * self.capacity, self.capacity), self.capacity)
            into[g, at, :] = part

    def combine(self, position, made, init, slots, sems, write):
        def start(g):
            return pltpu.make_async_copy(init.at[g], slots.at[g % 2], sems.at[g % 2])

        start(0).start()
        for g in range(self.groups):
            if g + 1 < self.groups:
                start(g + 1).start()
            found = [self.taken(position, k, g).astype(bf16) for k in range(self.held)]
            found = dot_rows(jnp.concatenate(found, axis=0), made[g])
            start(g).wait()
            write(g, found + slots[g % 2])


def experts_forward(position, gate, spots, capacity, tokens, shares, init):
    (held, groups, rows), (_, _, width, hidden) = position.shape, shares.shape
    cores, slots = spots.shape[1], groups * capacity
    plan = Experts(held, cores, groups, rows, capacity)

    def kernel(spots, position, gate, tokens, shares, init, out, work, pre, weight, rows_all, made, sums, sems, sum_sems):
        step = pl.program_id(0)
        plan.weights_of(step, spots, shares, weight, sems)

        @pl.when(step == 0)
        def _():
            plan.dispatch(position, tokens, rows_all)

        plan.wait_weights(step, spots, shares, weight, sems)
        slot = lax.rem(step, 2)
        mine = rows_all[step]
        work[0] = mine
        produced = 0.0
        for c in range(cores):
            pre_gate = product(mine, weight[slot, c, 0])
            pre_up = product(mine, weight[slot, c, 1])
            pre[0, c, 0], pre[0, c, 1] = pre_gate, pre_up
            act = (pre_gate * (1.0 / (1.0 + jnp.exp(-pre_gate))) * pre_up).astype(bf16)
            produced = produced + product_transposed(act, weight[slot, c, 2])
        plan.keep((produced * plan.scales(position, gate, step)).astype(bf16), step, made)

        @pl.when(step == held - 1)
        def _():
            def write(g, total):
                out[g] = total.astype(bf16)

            plan.combine(position, made, init, sums, sum_sems, write)

    whole = pl.BlockSpec(position.shape, lambda j: (0, 0, 0))
    return pl.pallas_call(
        kernel,
        grid=(held,),
        in_specs=[
            scalars,
            whole,
            whole,
            pl.BlockSpec(tokens.shape, lambda j: (0, 0), pipeline_mode=pl.Buffered(1)),
            anywhere,
            anywhere,
        ],
        out_specs=[
            pl.BlockSpec((groups, rows, width), lambda j: (0, 0, 0)),
            pl.BlockSpec((1, slots, width), lambda j: (j, 0, 0)),
            pl.BlockSpec((1, cores, 2, slots, hidden), lambda j: (j, 0, 0, 0, 0)),
        ],
        out_shape=[
            jax.ShapeDtypeStruct((groups, rows, width), bf16),
            jax.ShapeDtypeStruct((held, slots, width), bf16),
            jax.ShapeDtypeStruct((held, cores, 2, slots, hidden), f32),
        ],
        scratch_shapes=[
            pltpu.VMEM((2, cores, 3, width, hidden), bf16),
            pltpu.VMEM((held, slots, width), bf16),
            pltpu.VMEM((groups, held * capacity, width), bf16),
            pltpu.VMEM((2, rows, width), f32),
            pltpu.SemaphoreType.DMA((2, cores)),
            pltpu.SemaphoreType.DMA((2,)),
        ],
        compiler_params=room,
        cost_estimate=no_cost,
    )(spots, position, gate, tokens, shares, init.reshape(groups, rows, width))


def experts_backward(position, gate, spots, capacity, tokens, work, pre, shares, init):
    (held, groups, rows), (_, _, width, hidden) = position.shape, shares.shape
    cores, slots = spots.shape[1], groups * capacity
    plan = Experts(held, cores, groups, rows, capacity)

    def kernel(
        spots, position, gate, tokens, work, pre, shares, init, out, grads, weight, rows_all, made, sums, fresh,
        found, sems, sum_sems, out_sems,
    ):
        step = pl.program_id(0)
        plan.weights_of(step, spots, shares, weight, sems)

        @pl.when(step == 0)
        def _():
            plan.dispatch(position, tokens, rows_all)

        plan.wait_weights(step, spots, shares, weight, sems)
        slot = lax.rem(step, 2)
        scale = plan.scales(position, gate, step)
        mine, produced, chosen, acts, pres = rows_all[step], 0.0, 0.0, [], []
        for c in range(cores):
            back = product(mine, weight[slot, c, 2])
            pre_gate, pre_up = pre[0, c, 0], pre[0, c, 1]
            logistic = 1.0 / (1.0 + jnp.exp(-pre_gate))
            activated = pre_gate * logistic * pre_up
            chosen = chosen + jnp.sum(back * activated, axis=1, keepdims=True)
            acts.append((activated * scale).astype(bf16))
            back = back * scale
            grad_gate = back * pre_up * logistic * (1.0 + pre_gate * (1.0 - logistic))
            pres.append((grad_gate.astype(bf16), (back * pre_gate * logistic).astype(bf16)))
            for s in range(2):
                produced = produced + product_transposed(pres[c][s], weight[slot, c, s])
        plan.keep(produced.astype(bf16), step, made)
        for g in range(groups):
            taken = slot_matrix(position[step, pl.ds(g, 1), :], capacity)
            part = chosen[g * capacity : (g + 1) * capacity]
            found[step, pl.ds(g, 1), :] = jnp.sum(jnp.where(taken, part, 0.0), axis=0, keepdims=True)

        def store(k):
            return [
                pltpu.make_async_copy(fresh.at[c], grads.at[spots[k, c]], out_sems.at[c])
                for c in range(cores)
            ]

        for k in range(1, held):

            @pl.when(step == k)
            def _():
                for copy in store(k - 1):
                    copy.wait()

        for c in range(cores):
            both = dot_rows(work[0], jnp.concatenate(pres[c], axis=1)).astype(bf16)
            fresh[c, 0], fresh[c, 1] = both[:, :hidden], both[:, hidden:]
        both = dot_rows(mine, jnp.concatenate(acts, axis=1)).astype(bf16)
        for c in range(cores):
            fresh[c, 2] = both[:, c * hidden : (c + 1) * hidden]
        for k in range(held):

            @pl.when(step == k)
            def _():
                for copy in store(k):
                    copy.start()

        @pl.when(step == held - 1)
        def _():
            def write(g, total):
                out[g, pl.ds(0, rows), :] = total.astype(bf16)
                tail = jnp.concatenate([found[k, g : g + 1, :] for k in range(held)], axis=0)
                high = tail.astype(bf16).astype(f32)
                tail = [high, tail - high, jnp.zeros((TAIL - 2 * held, rows), f32)]
                out[g, pl.ds(rows, TAIL), pl.ds(0, rows)] = jnp.concatenate(tail, axis=0).astype(bf16)

            plan.combine(position, made, init, sums, sum_sems, write)
            for copy in store(held - 1):
                copy.wait()

    whole = pl.BlockSpec(position.shape, lambda j: (0, 0, 0))
    return pl.pallas_call(
        kernel,
        grid=(held,),
        in_specs=[
            scalars,
            whole,
            whole,
            pl.BlockSpec(tokens.shape, lambda j: (0, 0), pipeline_mode=pl.Buffered(1)),
            pl.BlockSpec((1, slots, width), lambda j: (j, 0, 0)),
            pl.BlockSpec((1, cores, 2, slots, hidden), lambda j: (j, 0, 0, 0, 0)),
            anywhere,
            anywhere,
        ],
        out_specs=[pl.BlockSpec((groups, rows + TAIL, width), lambda j: (0, 0, 0)), anywhere],
        out_shape=[
            jax.ShapeDtypeStruct((groups, rows + TAIL, width), bf16),
            jax.ShapeDtypeStruct(shares.shape, bf16),
        ],
        scratch_shapes=[
            pltpu.VMEM((2, cores, 3, width, hidden), bf16),
            pltpu.VMEM((held, slots, width), bf16),
            pltpu.VMEM((groups, held * capacity, width), bf16),
            pltpu.VMEM((2, rows, width), f32),
            pltpu.VMEM((cores, 3, width, hidden), bf16),
            pltpu.VMEM(position.shape, f32),
            pltpu.SemaphoreType.DMA((2, cores)),
            pltpu.SemaphoreType.DMA((2,)),
            pltpu.SemaphoreType.DMA((cores,)),
        ],
        compiler_params=room,
        cost_estimate=no_cost,
    )(spots, position, gate, tokens, work, pre, shares, init.reshape(groups, rows, width))


def spread_shared(lay, shared_in, shared_out, member):
    rows, hidden = shared_out.shape
    part = hidden // len(lay.g_masks)
    stacked = jnp.concatenate([shared_in, shared_out[None]], axis=0)
    stacked = stacked.reshape(3 * rows, hidden)
    member_rows = member.reshape(-1, part)

    def piece(mask):
        chunk = lax.dynamic_slice_in_dim(stacked, lay.chunk(mask) * part, part, 1)
        return jnp.concatenate([chunk, member_rows], axis=0)

    pieces = [piece(0)] + [lay.shift(piece(m), m) for m in lay.g_masks[1:]]
    chunks = jnp.stack([p[: 3 * rows].reshape(3, rows, part) for p in pieces])
    return chunks, jnp.stack([p[3 * rows :].reshape(member.shape) for p in pieces])


def gather_shared(lay, blocks):
    _, _, matrices, rows, part = (len(blocks),) + blocks[0].shape
    everyone = jnp.stack(blocks, axis=1)
    natural = everyone.reshape((lay.dp, matrices, rows, part))[lay.rows_order()]
    return natural.transpose(1, 0, 2, 3).reshape(matrices, lay.dp * rows, part)


def scatter_shared(lay, grads, after):
    part = grads.shape[2] // lay.tp
    rows = grads.shape[1] // lay.dp
    own = lay.scatter_core([grads[:, :, k * part : (k + 1) * part] for k in range(lay.tp)])
    natural = own.astype(bf16).reshape(3, lay.dp, rows, part).transpose(1, 0, 2, 3)
    blocks = natural[lay.rows_apart()].reshape(len(lay.g_masks), len(lay.w_masks), 3, rows, part)
    summed = lay.scatter_w([blocks[:, k] for k in range(len(lay.w_masks))], after[0])
    summed = behind(summed, after[2])
    out = jnp.zeros((3, rows, part * len(lay.g_masks)), f32)
    for k, mask in enumerate(lay.g_masks):
        got = summed[k] if k == 0 else lay.shift(summed[k].astype(bf16), mask).astype(f32)
        out = lax.dynamic_update_slice_in_dim(out, got, lay.chunk(mask) * part, 2)
    return out


def scatter_parts(lay, parts):
    return [lay.shift(part, mask) if mask else part for part, mask in zip(parts, lay.g_masks)]


def on_device(
    block_input,
    teacher,
    lengths,
    routes,
    gain_attn,
    w_query,
    key_value_weight,
    w_out,
    gain_moe,
    w_router,
    w_shared_in,
    w_shared_out,
    w_expert_in,
    w_expert_out,
):
    lay = Layout()
    own_rows, width = block_input.shape
    tp, dp = lay.tp, lay.dp
    sequence_length = own_rows * tp
    experts = w_expert_in.shape[0] * dp
    capacity = max(2, own_rows * TOPK * 4 // (3 * experts))
    n_g, n_w = len(lay.g_masks), len(lay.w_masks)
    length = lengths[lay.place]
    slices = jnp.array(range(tp), jnp.int32) ^ lay.core
    positions = (slices[:, None] * own_rows + jnp.arange(own_rows)[None, :]).reshape(-1)
    own_valid = (positions[:own_rows] < length).astype(f32)[:, None]
    head_count = w_query.shape[1] // HEAD_SIZE
    kv_count = key_value_weight.shape[2] // HEAD_SIZE
    head_group = head_count // kv_count
    q_dim, kv_dim = head_count * HEAD_SIZE, kv_count * HEAD_SIZE
    in_kernel = n_g * own_rows <= 1024
    forward = experts_forward if in_kernel else experts_forward_plain
    backward = experts_backward if in_kernel else experts_backward_plain

    near, far = (1 << bit for bit in lay.w_bits)
    qkv = Tree(lay, jnp.concatenate([w_query, key_value_weight[0], key_value_weight[1]], axis=1))
    router_pad = jnp.zeros((w_router.shape[0], -experts % 128), bf16)
    out = Tree(lay, jnp.concatenate([w_out, w_router, router_pad], axis=1))
    steps = len(lay.tree_bits)
    qkv.step()
    out.step(qkv.marks[0])
    qkv.step()
    input_slices = lay.gather_core(behind(block_input, qkv.marks[0]))

    own_routes = lax.dynamic_slice_in_dim(routes, lay.core * own_rows, own_rows, 0)
    expert_ids = jnp.arange(experts, dtype=jnp.int32)
    member = jnp.any(own_routes.T[None, :, :] == expert_ids[:, None, None], axis=1)
    held_ids = lay.place ^ jnp.array(lay.w_masks, jnp.int32)
    held_hot = (held_ids[:, None] == expert_ids).astype(f32)
    shared_parts, group_member = spread_shared(
        lay, *behind((w_shared_in, w_shared_out), qkv.marks[0]), member.astype(bf16)
    )
    held_member = contract("je,get->jgt", held_hot.astype(bf16), group_member)
    before = jnp.triu(jnp.ones((own_rows, own_rows), bf16), 1)
    position = contract("jgu,ut->jgt", held_member.astype(bf16), before)
    position = jnp.where(held_member > 0, position, -1.0)

    out.step(qkv.marks[1])
    for k in range(2, steps):
        qkv.step(out.marks[k - 2], *([shared_parts, input_slices] if k == 2 else []))
        out.step(qkv.marks[k])
    shared_far = lay.shift(behind(shared_parts, out.marks[0]), far)
    expert_shares = lax.all_gather(
        behind(jnp.concatenate([w_expert_in[0], w_expert_out], axis=0), qkv.marks[2], shared_far),
        ("dp", "tensor"),
        axis_index_groups=lay.w_groups(),
    )
    shared_near = lay.shift(behind(jnp.stack([shared_parts, shared_far]), out.marks[-2]), near)

    spot = jnp.stack([lay.core, length]).astype(jnp.int32)
    in_order = lay.tree_order()
    residual = block_input.astype(f32)
    _, scale_attn = normalize_rows(residual, gain_attn)

    def by_core(rows):
        return [rows[k * own_rows : (k + 1) * own_rows] for k in range(tp)]

    if in_kernel:
        normed_all, projected, mixed_heads, logs = attend(
            in_order, spot, *input_slices, gain_attn, qkv.halves, head_count, kv_count
        )
        *attn_parts, out_router = project_out(
            in_order, mixed_heads, out.halves
        )
    else:
        qkv_full, out_router = lay.in_order(qkv.halves), lay.in_order(out.halves)
        normed_all, _ = normalize_rows(
            jnp.concatenate(input_slices, axis=0).astype(f32), gain_attn
        )
        projected = product(normed_all, qkv_full).astype(bf16)
        queries = projected[:, :q_dim].reshape(sequence_length, kv_count, head_group, HEAD_SIZE)
        key_row_table = projected[:, q_dim : q_dim + kv_dim].reshape(
            sequence_length, kv_count, HEAD_SIZE
        )
        value_row_table = projected[:, q_dim + kv_dim :].reshape(
            sequence_length, kv_count, HEAD_SIZE
        )
        allowed = (positions[None, :] <= positions[:, None]) & (positions[None, :] < length)
        scores = contract("qvgd,kvd->vgqk", queries, key_row_table) * HEAD_SIZE ** (-0.5)
        scores = jnp.where(allowed, scores, masked_score)
        row_max = jnp.max(scores, axis=-1, keepdims=True)
        exponent_terms = jnp.exp(scores - row_max)
        row_sum = jnp.sum(exponent_terms, axis=-1, keepdims=True)
        probs_full = exponent_terms / row_sum
        probs_low = probs_full.astype(bf16)
        mixed_heads = (
            contract("vgqk,kvd->qvgd", probs_low, value_row_table)
            .astype(bf16)
            .reshape(sequence_length, q_dim)
        )
        attn_parts = by_core(product_transposed(mixed_heads, out_router[:, :q_dim]))
    router_full = out_router[:, q_dim : q_dim + experts]
    hidden = residual + lay.scatter_core(attn_parts)
    moe_own, scale_moe = normalize_rows(hidden, gain_moe)

    arrived = lay.gather_g(moe_own)
    shared_near = behind(shared_near, arrived[1])
    shared_own = gather_shared(lay, [shared_parts, shared_near[0], shared_far, shared_near[1]])
    shared_full = jnp.concatenate(lay.gather_core(shared_own), axis=2)
    shared_in_full, shared_out_full = shared_full[:2], shared_full[2]

    group_rows = jnp.concatenate(arrived, axis=0)
    logits = lax.dot_general(
        router_full, group_rows, (((0,), (1,)), ((), ())), preferred_element_type=f32
    )
    shown = jnp.where(
        group_member.transpose(1, 0, 2).reshape(experts, -1) > 0, logits, masked_score
    )
    gate_terms = jnp.exp(shown - jnp.max(shown, axis=0, keepdims=True))
    gates = gate_terms / jnp.sum(gate_terms, axis=0, keepdims=True)
    own_gates = gates[:, :own_rows]
    held_gates = jnp.sum(held_hot[:, :, None] * gates[None], axis=1).reshape(n_w, n_g, own_rows)
    shared_pre = contract("td,cdf->ctf", group_rows, shared_in_full)
    shared_act = (jax.nn.silu(shared_pre[0]) * shared_pre[1]).astype(bf16)
    total = product_transposed(shared_act, shared_out_full)
    spots = lay.w_spots()
    total, work, pre = forward(
        position, held_gates, spots, capacity, group_rows, expert_shares, total
    )

    def scatter_g(parts):
        return sum(part.astype(f32) for part in scatter_parts(lay, parts))

    out_rows = (hidden + scatter_g([total[k] for k in range(n_g)])) * own_valid
    residual_error = (out_rows - teacher.astype(f32)) * own_valid
    loss_part = 0.5 * jnp.sum(residual_error * residual_error)

    group_grad = jnp.concatenate(lay.gather_g(residual_error.astype(bf16)), axis=0)
    grad_shared_act = product(group_grad, shared_out_full)
    grad_shared_out = product_left(group_grad, shared_act)
    grad_shared_pre = jnp.stack(swish_back(shared_pre[0], shared_pre[1], grad_shared_act))
    grad_shared_in = contract("td,ctf->cdf", group_rows, grad_shared_pre)
    total = contract("ctf,cdf->td", grad_shared_pre, shared_in_full)
    total, grad_shares = backward(
        position, held_gates, spots, capacity, group_grad, work, pre, expert_shares, total
    )
    grad_expert = lax.psum_scatter(
        grad_shares, ("dp", "tensor"), axis_index_groups=lay.w_groups()
    ).astype(f32)
    received = scatter_parts(lay, [total[k] for k in range(n_g)])
    returned = received[0][:own_rows].astype(f32)
    for part in received[1:]:
        returned = returned + part[:own_rows].astype(f32)
    gate_rows = [part[own_rows:, :own_rows].astype(f32) for part in received]
    gate_rows = [rows[:n_w] + rows[n_w : 2 * n_w] for rows in gate_rows]
    ids = lay.place ^ jnp.array([g ^ w for g in lay.g_masks for w in lay.w_masks], jnp.int32)
    placed = (expert_ids[:, None] == ids).astype(f32)[:, :, None]
    grad_gates = jnp.sum(placed * jnp.concatenate(gate_rows, axis=0)[None], axis=1)
    grad_logits = (
        own_gates * (grad_gates - jnp.sum(own_gates * grad_gates, axis=0, keepdims=True))
    ).astype(bf16)
    grad_router_part = lax.dot_general(
        moe_own, grad_logits, (((0,), (1,)), ((), ())), preferred_element_type=f32
    )
    grad_normed_own = returned + lax.dot_general(
        grad_logits, router_full, (((0,), (1,)), ((), ())), preferred_element_type=f32
    )

    grad_from_moe, grad_gain_moe_part = normalize_back(hidden, scale_moe, gain_moe, grad_normed_own)
    grad_hidden = residual_error + grad_from_moe
    grad_slices = lay.gather_core(grad_hidden.astype(bf16))
    grad_router_part = jnp.pad(
        lay.scatter_core([grad_router_part] * tp).astype(bf16), ((0, 0), (0, -experts % 128))
    )
    if in_kernel:
        grad_mixed, *out_back_halves = project_out_back(
            lay.tree_order(), *grad_slices, out_router, mixed_heads, grad_router_part
        )
        grad_projected, *qkv_back_halves = attend_back(
            lay.tree_order(), spot, grad_mixed, normed_all, projected, logs, head_count, kv_count
        )
        normed_parts = normed_back(in_order, grad_projected, qkv.halves)
    else:
        grad_attn = jnp.concatenate(grad_slices, axis=0)
        grad_mixed = (
            product(grad_attn, out_router[:, :q_dim])
            .astype(bf16)
            .reshape(sequence_length, kv_count, head_group, HEAD_SIZE)
        )
        grad_values = contract("vgqk,qvgd->kvd", probs_low, grad_mixed)
        grad_probs = contract("qvgd,kvd->vgqk", grad_mixed, value_row_table)
        delta_sum = jnp.sum(probs_full * grad_probs, axis=-1, keepdims=True)
        grad_scores = (probs_full * (grad_probs - delta_sum)).astype(bf16)
        grad_queries = contract("vgqk,kvd->qvgd", grad_scores, key_row_table) * HEAD_SIZE ** (-0.5)
        grad_keys = contract("vgqk,qvgd->kvd", grad_scores, queries) * HEAD_SIZE ** (-0.5)
        grad_projected = jnp.concatenate(
            [
                grad_queries.astype(bf16).reshape(sequence_length, q_dim),
                grad_keys.astype(bf16).reshape(sequence_length, kv_dim),
                grad_values.astype(bf16).reshape(sequence_length, kv_dim),
            ],
            axis=1,
        )
        out_back_halves = lay.in_halves(
            jnp.concatenate([product_left(grad_attn, mixed_heads).astype(bf16), grad_router_part], axis=1)
        )
        qkv_back_halves = lay.in_halves(product_left(normed_all, grad_projected))
        normed_parts = by_core(product_transposed(grad_projected, qkv_full))
    out_back = Sum(lay, out_back_halves)
    keep, send = qkv_back_halves
    send = behind(send, out_back.step(grad_projected))
    qkv_back = Sum(lay, (keep, send))
    qkv_back.step()
    for k in range(1, steps):
        out_back.step(qkv_back.marks[k - 1] if k > 1 else grad_projected)
        qkv_back.step()
    grad_qkv, grad_out_router = qkv_back.total[0], out_back.total[0]
    qkv_back = qkv_back.marks
    grad_normed_attn = lay.scatter_core(normed_parts)
    grad_from_attn, grad_gain_attn_part = normalize_back(
        residual, scale_attn, gain_attn, grad_normed_attn
    )
    input_grad = grad_hidden + grad_from_attn
    grad_w_kv = jnp.stack(
        [grad_qkv[:, q_dim : q_dim + kv_dim], grad_qkv[:, q_dim + kv_dim :]], axis=0
    )
    small = jnp.stack(
        [grad_gain_attn_part, grad_gain_moe_part, jnp.full((width,), loss_part, f32)], axis=0
    )
    small = lay.sum_all(small, qkv_back)
    loss = small[2, 0] / (jnp.sum(lengths).astype(f32) * width)
    grad_shared = scatter_shared(
        lay, jnp.concatenate([grad_shared_in, grad_shared_out[None]]), qkv_back
    )
    return (
        out_rows.astype(bf16),
        loss,
        input_grad,
        small[0],
        grad_qkv[:, :q_dim],
        grad_w_kv,
        grad_out_router[:, :q_dim],
        small[1],
        grad_out_router[:, q_dim : q_dim + experts],
        grad_shared[:2],
        grad_shared[2],
        grad_expert[None, :2],
        grad_expert[2:],
    )


def solution(mesh):
    rows, weights = P(("dp", "tensor"), None), P("dp", "tensor")
    stacked = P(None, "dp", "tensor")
    expert_in, expert_out = P("dp", None, None, "tensor"), P("dp", None, "tensor")
    return jax.shard_map(
        on_device,
        mesh=mesh,
        in_specs=(
            rows,
            rows,
            P(),
            P("dp", None),
            P(),
            weights,
            stacked,
            weights,
            P(),
            P("dp", None),
            stacked,
            weights,
            expert_in,
            expert_out,
        ),
        out_specs=(
            rows,
            P(),
            rows,
            P(),
            weights,
            stacked,
            weights,
            P(),
            P("dp", None),
            stacked,
            weights,
            expert_in,
            expert_out,
        ),
        check_vma=False,
    )
```
